256 devices in a mesh: blk: 16 (over y, x_lo, core), inner: 16 (over x_hi, z).
Axes of the slice: x: 4 (x_hi: 2, x_lo: 2; x = x_hi * 2 + x_lo), y: 4, z: 8, core: 2. Of those that a mesh axis runs over, the one named last changes fastest.
Arguments:
- records: float32 [2048, 64, 2048], P('blk', 'inner'), may hold values from -6 to 6
- starts: int32 [64], P('inner'), may hold values from 0 to 1024, as said below
- offsets: int32 [2048, 16], P('blk'), may hold values from -256 to 256, as said below
Outputs:
- correlations: float32 [16, 2048, 768], P('inner', 'blk')
The draws below stay inside these ranges and needn't reach their ends.
Inputs may be any that keep to these rules, and one draw needn't show every extreme that they name: Segment s uses samples starts[s] to starts[s] + 1023 of its slot. `offsets`: never zero; the partner of channel c is (c + offset) mod 2048.
All inputs are finite; a program needn't handle non-finite values.
Results may differ from the reference program's by a relative error of at most 0.0003.
Values sent between devices are 32-bit elements; how exact they have to be, the bound alone decides.
A program may use at most 128 MiB of HBM per device.

```python
import math
import jax
import jax.numpy as jnp
from jax import lax

SEG = 1024
SLOT = 2048
LAGS = 768
HALF = 32
PAIRS = 16
F = 512
SEP = 256
CHANNELS = 2048
SEGS = 64


def draw_starts(key, part):
    values = jax.random.randint(key, (SEGS,), 0, SLOT - SEG + 1)
    values = values.at[0].set(0).at[1].set(SLOT - SEG)
    return values.astype(jnp.int32)


def draw_offsets(key, part):
    first_key, second_key = jax.random.split(key)
    magnitude = jax.random.randint(first_key, (CHANNELS, PAIRS), 1, SEP + 1)
    direction = jax.random.randint(second_key, (CHANNELS, PAIRS), 0, 2) * 2 - 1
    values = magnitude * direction
    values = values.at[0, 0].set(SEP).at[1, 0].set(-SEP)
    return values.astype(jnp.int32)


def steps_of(stream_key, shape, cuts, smallest, top_value):
    gain, own = 1.0, jax.random.fold_in(stream_key, 6)
    for position, shards_of in cuts:
        draws = jnp.exp(jax.random.uniform(jax.random.fold_in(own, position), (shards_of,), jnp.float32, smallest / len(cuts), top_value / len(cuts)))
        gain = gain * jnp.repeat(draws, shape[position] // shards_of).reshape([-1 if axis == position else 1 for axis in range(len(shape))])
    return gain


def gaussian(key, shape, width, most, cuts=(), held_as=jnp.bfloat16):
    values = width * jax.random.normal(key, shape, jnp.float32)
    if cuts:
        values = values * steps_of(key, shape, cuts, -0.22, 0.18)
    return jnp.clip(values, -most, most).astype(held_as)


def setup_inputs(seed: int = 0) -> dict:
    seeds = jax.random.split(jax.random.key(seed), 4)
    records = gaussian(seeds[0], (CHANNELS, SEGS, SLOT), 1.0, 6.0, ((0, 16), (1, 16)), jnp.float32)
    starts = draw_starts(jax.random.fold_in(seeds[3], 71), 0)
    offsets = draw_offsets(jax.random.fold_in(seeds[3], 71), 0)
    return {"records": records, "starts": starts, "offsets": offsets}


def lag_table():
    bins = jnp.arange(F, dtype=jnp.int32)
    shifts = jnp.arange(LAGS, dtype=jnp.int32) - LAGS // 2
    phase = bins[:, None] * shifts[None, :] % SEG
    angle = 2.0 * jnp.pi / SEG * phase.astype(jnp.float32)
    table = jnp.concatenate([jnp.cos(angle), -jnp.sin(angle)], 0)
    return (table * math.sqrt(SEGS / F)).astype(jnp.float32)

def reference(records, starts, offsets):
    samples = jnp.arange(SEG, dtype=jnp.int32).astype(jnp.float32)
    window = (0.5 - 0.5 * jnp.cos(2.0 * jnp.pi * samples / SEG)).astype(jnp.float32)
    bins = jnp.arange(F, dtype=jnp.int32)
    distance = jnp.abs(bins[:, None] - bins[None, :])
    distance = jnp.minimum(distance, F - distance)
    band = ((distance <= HALF).astype(jnp.float32) / (2 * HALF + 1)).astype(jnp.float32)

    def one_segment(inputs):
        slot_rows, begin = inputs
        pieces = lax.dynamic_slice_in_dim(slot_rows, begin.astype(jnp.int32), SEG, 1) * window
        spectrum = jnp.fft.rfft(pieces, axis=1)[:, :F]
        spec_re = jnp.real(spectrum).astype(jnp.float32)
        spec_im = jnp.imag(spectrum).astype(jnp.float32)
        power = spec_re * spec_re + spec_im * spec_im
        smooth = jnp.dot(power, band, precision=lax.Precision.HIGHEST, preferred_element_type=jnp.float32)
        scale = lax.rsqrt(smooth + 1e-06)
        return (spec_re * scale, spec_im * scale)
    white_re, white_im = lax.map(one_segment, (jnp.moveaxis(records, 1, 0), starts))
    table = lag_table()
    channel_ids = jnp.arange(CHANNELS, dtype=jnp.int32)

    def one_pair(column):
        partner = (channel_ids + offsets[:, column]) % CHANNELS
        partner_re = white_re[:, partner, :]
        partner_im = white_im[:, partner, :]
        cross_re = lax.optimization_barrier(jnp.sum(white_re * partner_re + white_im * partner_im, axis=0)) / SEGS
        cross_im = lax.optimization_barrier(jnp.sum(white_im * partner_re - white_re * partner_im, axis=0)) / SEGS
        joined = jnp.concatenate([cross_re, cross_im], 1)
        return jnp.dot(joined, table, precision=lax.Precision.HIGHEST, preferred_element_type=jnp.float32)
    return lax.map(one_pair, jnp.arange(PAIRS, dtype=jnp.int32))
```

```python
import math

import ml_dtypes
import numpy as np

import jax
import jax.numpy as jnp
from jax import lax
from jax.experimental import pallas as pl
from jax.experimental.pallas import tpu as pltpu
from jax.sharding import PartitionSpec as P

SEG = 1024
SLOT = 2048
LAGS = 768
HALF = 32
PAIRS = 16
F = 512
SEP = 256
CUT = SEG + 128
LANES = 128


def split_table():
    samples = np.arange(SEG // 2, dtype=np.int64)
    rows = []
    for parity in range(2):
        bins = 2 * np.arange(F // 2, dtype=np.int64) + parity
        angle = 2.0 * np.pi / SEG * (bins[:, None] * samples[None, :] % SEG)
        rows += [np.cos(angle), -np.sin(angle)]
    table = np.concatenate(rows, 0).astype(np.float32)
    high = table.astype(ml_dtypes.bfloat16)
    low = (table - high.astype(np.float32)).astype(ml_dtypes.bfloat16)
    return high, low


def split(value):
    high = value.astype(jnp.bfloat16)
    low = (value - high.astype(jnp.float32)).astype(jnp.bfloat16)
    return high, low


def dot3(left, right, dims):
    left_high, left_low = left
    right_high, right_low = right

    def one(a, b):
        return lax.dot_general(a, b, (dims, ((), ())), preferred_element_type=jnp.float32)

    return one(left_high, right_high) + (one(left_high, right_low) + one(left_low, right_high))


def whiten_kernel(starts_ref, window_ref, high_ref, low_ref, records_ref, out_ref, cut_ref, band_ref, sems):
    segments = records_ref.shape[1]
    half = SEG // 2
    quarter = F // 2

    def copy(segment):
        first = lax.min(starts_ref[segment] // LANES, (SLOT - CUT) // LANES) * LANES
        return pltpu.make_async_copy(
            records_ref.at[:, segment, pl.ds(pl.multiple_of(first, LANES), CUT)],
            cut_ref.at[segment],
            sems.at[segment],
        )

    for segment in range(segments):
        copy(segment).start()
    row_ids = lax.broadcasted_iota(jnp.int32, (F, F), 0)
    column_ids = lax.broadcasted_iota(jnp.int32, (F, F), 1)
    row_bins = row_ids % quarter * 2 + row_ids // quarter
    column_bins = column_ids % quarter * 2 + column_ids // quarter
    distance = jnp.abs(row_bins - column_bins)
    distance = jnp.minimum(distance, F - distance)
    band_ref[...] = jnp.where(distance <= HALF, 1.0, 0.0).astype(jnp.bfloat16)
    contract_last = ((1,), (1,))
    for segment in range(segments):
        copy(segment).wait()
        begin = starts_ref[segment]
        first = lax.min(begin // LANES, (SLOT - CUT) // LANES) * LANES
        rolled = pltpu.roll(cut_ref[segment], lax.rem(CUT - (begin - first), CUT), 1)
        piece = rolled[:, :SEG] * window_ref[...]
        folded = (split(piece[:, :half] + piece[:, half:]), split(piece[:, :half] - piece[:, half:]))
        parts = []
        for parity in range(2):
            rows = pl.ds(parity * 2 * quarter, 2 * quarter)
            parts.append(dot3((high_ref[rows, :], low_ref[rows, :]), folded[parity], contract_last))
        power = jnp.concatenate(
            [part[:quarter] * part[:quarter] + part[quarter:] * part[quarter:] for part in parts], 0
        )
        power_high, power_low = split(power)
        band = band_ref[...]
        smooth = jnp.dot(band, power_high, preferred_element_type=jnp.float32) + jnp.dot(
            band, power_low, preferred_element_type=jnp.float32
        )
        scale = lax.rsqrt(smooth * (1.0 / (2 * HALF + 1)) + 1e-06)
        for parity in range(2):
            part_scale = scale[parity * quarter : (parity + 1) * quarter]
            for component in range(2):
                row = (parity * 2 + component) * segments + segment
                value = parts[parity][component * quarter : (component + 1) * quarter] * part_scale
                out_ref[pl.ds(row, quarter, stride=4 * segments), :] = value


def pair_kernel(offsets_ref, white_ref, out_ref, high_ref, low_ref, left_high_ref, left_low_ref, gram_ref):
    blocks, rows, channels = white_ref.shape
    segments = 4
    row_ids = lax.broadcasted_iota(jnp.int32, (rows, channels), 0)
    component = row_ids // segments % 4
    is_imag = component % 2 == 1
    parity = component // 2
    reach = SEP // channels
    width = (2 * reach + 1) * channels

    def fill(block, _):
        value = white_ref[block]
        high, low = split(value)
        high_ref[block] = high
        low_ref[block] = low
        up = pltpu.roll(value, rows - segments, 0)
        down = pltpu.roll(value, segments, 0)
        swapped = jnp.where(is_imag, -down, up)
        high_swapped, low_swapped = split(swapped)
        zero = jnp.zeros_like(high)
        for which in range(2):
            keep = parity == which
            left_high_ref[block, :, pl.ds(which * 2 * channels, channels)] = jnp.where(keep, high, zero)
            left_low_ref[block, :, pl.ds(which * 2 * channels, channels)] = jnp.where(keep, low, zero)
            left_high_ref[block, :, pl.ds((which * 2 + 1) * channels, channels)] = jnp.where(
                keep, high_swapped, zero
            )
            left_low_ref[block, :, pl.ds((which * 2 + 1) * channels, channels)] = jnp.where(
                keep, low_swapped, zero
            )
        return 0

    lax.fori_loop(0, blocks, fill, 0)
    lane_ids = lax.broadcasted_iota(jnp.int32, (channels, channels), 1)
    group = lane_ids // PAIRS
    contract_first = ((0,), (0,))

    def one_block(block, _):
        left = (left_high_ref[block], left_low_ref[block])
        index = offsets_ref[block]
        where_block = index // channels
        lane = index % channels
        picked = jnp.zeros((channels, channels), jnp.float32)
        for step in range(2 * reach + 1):
            other = lax.rem(block + blocks + step - reach, blocks)
            gram = dot3(left, (high_ref[other], low_ref[other]), contract_first)
            hit = where_block == step
            for which in range(4):
                found = jnp.take_along_axis(
                    gram[which * channels : (which + 1) * channels], lane, axis=1, mode="promise_in_bounds"
                )
                picked = jnp.where(hit & (group == which), found, picked)
        out_ref[block] = picked.T[: 4 * PAIRS]
        return 0

    lax.fori_loop(0, blocks, one_block, 0)


def lag_kernel(high_ref, low_ref, cross_ref, out_ref):
    half = SEG // 2
    quarter = F // 2
    sums = []
    for parity in range(2):
        total = None
        for component in range(2):
            place = parity * 2 + component
            value = split(cross_ref[pl.ds(place, quarter, stride=4), :])
            rows = pl.ds(place * quarter, quarter)
            term = dot3(value, (high_ref[rows, :], low_ref[rows, :]), ((0,), (0,)))
            total = term if total is None else total + term
        sums.append(total)
    even, odd = sums
    shift = LAGS // 2
    out_ref[0, :, pl.ds(0, shift)] = (even - odd)[:, half - shift :]
    out_ref[0, :, pl.ds(shift, shift)] = (even + odd)[:, :shift]


def local(records, starts, offsets):
    channels, segments, _ = records.shape
    blocks = lax.axis_size("blk")
    inner = lax.axis_size("inner")
    devices = blocks * inner
    rows = 4 * segments
    high, low = split_table()
    high, low = jnp.asarray(high), jnp.asarray(low)
    samples = np.arange(SEG)
    window = jnp.asarray((0.5 - 0.5 * np.cos(2.0 * np.pi * samples / SEG)).astype(np.float32)[None, :])
    vmem = pl.BlockSpec(memory_space=pltpu.VMEM)
    smem = pl.BlockSpec(memory_space=pltpu.SMEM)
    white = pl.pallas_call(
        whiten_kernel,
        out_shape=jax.ShapeDtypeStruct((devices * rows, channels), jnp.float32),
        in_specs=[smem, vmem, vmem, vmem, pl.BlockSpec(memory_space=pl.ANY)],
        out_specs=vmem,
        scratch_shapes=[
            pltpu.VMEM((segments, channels, CUT), jnp.float32),
            pltpu.VMEM((F, F), jnp.bfloat16),
            pltpu.SemaphoreType.DMA((segments,)),
        ],
        compiler_params=pltpu.CompilerParams(vmem_limit_bytes=40 << 20),
    )(starts, window, high, low, records)
    axes = ("blk", "inner")
    white = lax.all_to_all(white.reshape(devices, rows, channels), axes, split_axis=0, concat_axis=0, tiled=True)
    place = offsets + (jnp.arange(channels, dtype=jnp.int32) + SEP)[:, None]
    place = lax.all_gather(place, "blk", axis=0, tiled=True).reshape(blocks, channels, PAIRS)
    place = jnp.tile(place, (1, 1, channels // PAIRS))
    cross = pl.pallas_call(
        pair_kernel,
        out_shape=jax.ShapeDtypeStruct((blocks, 4 * PAIRS, channels), jnp.float32),
        in_specs=[vmem, vmem],
        out_specs=vmem,
        scratch_shapes=[
            pltpu.VMEM((blocks, inner * rows, channels), jnp.bfloat16),
            pltpu.VMEM((blocks, inner * rows, channels), jnp.bfloat16),
            pltpu.VMEM((blocks, inner * rows, 4 * channels), jnp.bfloat16),
            pltpu.VMEM((blocks, inner * rows, 4 * channels), jnp.bfloat16),
            pltpu.VMEM((8, 128), jnp.float32),
        ],
        compiler_params=pltpu.CompilerParams(vmem_limit_bytes=40 << 20),
    )(place, white.reshape(blocks, inner * rows, channels))
    cross = cross.reshape(blocks, 4, PAIRS, channels).transpose(0, 2, 1, 3).reshape(devices, 4, channels)
    segment_count = inner * segments
    cross = cross * (math.sqrt(segment_count / F) / segment_count)
    cross = lax.all_to_all(cross, axes, split_axis=0, concat_axis=0, tiled=True)
    return pl.pallas_call(
        lag_kernel,
        out_shape=jax.ShapeDtypeStruct((1, channels, LAGS), jnp.float32),
        in_specs=[vmem, vmem, vmem],
        out_specs=vmem,
        compiler_params=pltpu.CompilerParams(vmem_limit_bytes=40 << 20),
    )(high, low, cross.reshape(devices * 4, channels))


def solution(mesh):
    placed = (P("blk", "inner", None), P("inner"), P("blk", None))
    return jax.shard_map(
        local, mesh=mesh, in_specs=placed, out_specs=P("inner", "blk", None), check_vma=False
    )
```

```python
import math

import ml_dtypes
import numpy as np

import jax
import jax.numpy as jnp
from jax import lax
from jax.experimental import pallas as pl
from jax.experimental.pallas import tpu as pltpu
from jax.sharding import PartitionSpec as P

SEG = 1024
SLOT = 2048
LAGS = 768
HALF = 32
PAIRS = 16
F = 512
SEP = 256
LANES = 128
CUT = SEG + LANES
BLOCKS = 16
INNER = 16
DEVICES = BLOCKS * INNER
SEGMENTS = 4
ROWS = 4 * SEGMENTS
QUARTER = F // 2
REACH = SEP // LANES
SPAN = 2 * REACH + 1
AHEAD = 6
MESH = pl.DeviceIdType.MESH


def split_table():
    samples = np.arange(SEG // 2, dtype=np.int64)
    rows = []
    for parity in range(2):
        bins = 2 * np.arange(QUARTER, dtype=np.int64) + parity
        angle = 2.0 * np.pi / SEG * (bins[:, None] * samples[None, :] % SEG)
        rows += [np.cos(angle), -np.sin(angle)]
    table = np.concatenate(rows, 0).astype(np.float32)
    high = table.astype(ml_dtypes.bfloat16)
    low = (table - high.astype(np.float32)).astype(ml_dtypes.bfloat16)
    return high, low


def split(value):
    high = value.astype(jnp.bfloat16)
    low = (value - high.astype(jnp.float32)).astype(jnp.bfloat16)
    return high, low


def dot(left, right, dims):
    return lax.dot_general(left, right, (dims, ((), ())), preferred_element_type=jnp.float32)


def cut_kernel(starts_hbm, records_ref, out_ref, starts_ref, cut_ref, starts_sem, sems):
    load = pltpu.make_async_copy(starts_hbm, starts_ref, starts_sem)
    load.start()
    load.wait()

    def first_of(segment):
        return lax.min(starts_ref[segment] // LANES, (SLOT - CUT) // LANES) * LANES

    def copy(segment):
        return pltpu.make_async_copy(
            records_ref.at[:, segment, pl.ds(pl.multiple_of(first_of(segment), LANES), CUT)],
            cut_ref.at[segment],
            sems.at[segment],
        )

    for segment in range(SEGMENTS):
        copy(segment).start()
    samples = lax.broadcasted_iota(jnp.int32, (8, SEG), 1).astype(jnp.float32)
    window = (0.5 - 0.5 * jnp.cos(2.0 * jnp.pi / SEG * samples))[:1]
    for segment in range(SEGMENTS):
        copy(segment).wait()
        shift = starts_ref[segment] - first_of(segment)
        rolled = pltpu.roll(cut_ref[segment], lax.rem(CUT - shift, CUT), 1)
        out_ref[segment] = rolled[:, :SEG] * window


def kernel(
    offsets_hbm,
    slots_ref,
    high_ref,
    low_ref,
    out_ref,
    offsets_ref,
    table_ref,
    band_ref,
    send_ref,
    recv_ref,
    place_ref,
    places_ref,
    right_ref,
    found_ref,
    cross_ref,
    offsets_sem,
    table_sems,
    local_sems,
    send_sems,
    recv_sems,
    place_sems,
    cross_sem,
):
    my_block = lax.axis_index("blk")
    my_inner = lax.axis_index("inner")
    me = my_block * INNER + my_inner
    half = SEG // 2

    def load_table(part):
        source = (high_ref, high_ref, low_ref)[part]
        return pltpu.make_async_copy(source, table_ref.at[:, pl.ds(part * half, half)], table_sems.at[part])

    load_offsets = pltpu.make_async_copy(offsets_hbm, offsets_ref, offsets_sem)
    load_offsets.start()
    for part in range(3):
        load_table(part).start()

    barrier = pltpu.get_barrier_semaphore()

    def greet(step, _):
        device = lax.rem(me + step, DEVICES)
        pl.semaphore_signal(
            barrier, inc=1, device_id=(device // INNER, lax.rem(device, INNER)), device_id_type=MESH
        )
        return 0

    lax.fori_loop(1, DEVICES, greet, 0, unroll=5)

    load_offsets.wait()
    channel_ids = lax.broadcasted_iota(jnp.int32, (1, LANES), 1)
    for pair in range(PAIRS):
        row = offsets_ref[pl.ds(pair, 1), :] + (channel_ids + SEP)
        place_ref[pl.ds(4 * pair, 4), :] = jnp.broadcast_to(row, (4, LANES))

    row_ids = lax.broadcasted_iota(jnp.int32, (F, F), 0)
    column_ids = lax.broadcasted_iota(jnp.int32, (F, F), 1)
    row_bins = row_ids % QUARTER * 2 + row_ids // QUARTER
    column_bins = column_ids % QUARTER * 2 + column_ids // QUARTER
    distance = jnp.abs(row_bins - column_bins)
    distance = jnp.minimum(distance, F - distance)
    band = jnp.where(distance <= HALF, 1.0, 0.0).astype(jnp.bfloat16)
    band_ref[:, pl.ds(0, F)] = band
    band_ref[:, pl.ds(F, F)] = band
    for part in range(3):
        load_table(part).wait()

    for first_segment in range(0, SEGMENTS, 2):
        pieces = []
        for segment in range(first_segment, first_segment + 2):
            pieces.append(slots_ref[segment])
        piece = jnp.concatenate(pieces, 0)
        parts = []
        for parity in range(2):
            front, back = piece[:, :half], piece[:, half:]
            high, low = split(front + back if parity == 0 else front - back)
            stacked = jnp.concatenate([high, low, high], 1)
            rows = table_ref[pl.ds(parity * 2 * QUARTER, 2 * QUARTER), :]
            parts.append(dot(rows, stacked, ((1,), (1,))))
        power = jnp.concatenate(
            [part[:QUARTER] * part[:QUARTER] + part[QUARTER:] * part[QUARTER:] for part in parts], 0
        )
        smooth = dot(band_ref[...], jnp.concatenate(split(power), 0), ((1,), (0,)))
        scale = lax.rsqrt(smooth * (1.0 / (2 * HALF + 1)) + 1e-06)
        for parity in range(2):
            part_scale = scale[parity * QUARTER : (parity + 1) * QUARTER]
            for component in range(2):
                value = parts[parity][component * QUARTER : (component + 1) * QUARTER] * part_scale
                for second in range(2):
                    row = (parity * 2 + component) * SEGMENTS + first_segment + second
                    send_ref[pl.ds(row, QUARTER, stride=ROWS), :] = value[:, second * LANES : (second + 1) * LANES]

    pl.semaphore_wait(barrier, DEVICES - 1)

    def chunk(device):
        return pl.ds(pl.multiple_of(device * ROWS, ROWS), ROWS)

    own_chunk = pltpu.make_async_copy(send_ref.at[chunk(me)], recv_ref.at[chunk(me)], local_sems.at[0])
    own_chunk.start()
    own_place = pltpu.make_async_copy(place_ref, places_ref.at[my_block], local_sems.at[1])
    own_place.start()

    def send_step(step):
        block = lax.rem(my_block + step, BLOCKS)

        def send_one(shift, _):
            other = lax.rem(my_inner + shift, INNER)
            pltpu.make_async_remote_copy(
                src_ref=send_ref.at[chunk(block * INNER + other)],
                dst_ref=recv_ref.at[chunk(me)],
                send_sem=send_sems.at[0],
                recv_sem=recv_sems.at[step],
                device_id=(block, other),
                device_id_type=MESH,
            ).start()
            return 0

        lax.fori_loop(1, INNER, send_one, 0)

        @pl.when(step > 0)
        def _():
            send_one(0, 0)
            pltpu.make_async_remote_copy(
                src_ref=place_ref,
                dst_ref=places_ref.at[my_block],
                send_sem=send_sems.at[1],
                recv_sem=place_sems.at[step],
                device_id=(block, my_inner),
                device_id_type=MESH,
            ).start()

    next_device = (lax.rem(my_block + 1, BLOCKS), my_inner)

    def awaited(source, target, send_sem, recv_sem):
        return pltpu.make_async_remote_copy(
            src_ref=source,
            dst_ref=target,
            send_sem=send_sem,
            recv_sem=recv_sem,
            device_id=next_device,
            device_id_type=MESH,
        )

    block_rows = INNER * ROWS
    lanes = lax.broadcasted_iota(jnp.int32, (LANES, LANES), 1)
    flips = lax.broadcasted_iota(jnp.int32, (INNER, 2 * SEGMENTS, LANES), 1) < SEGMENTS

    def block_of(step):
        return lax.rem(my_block + BLOCKS - step, BLOCKS)

    def block_values(block):
        values = recv_ref[pl.ds(pl.multiple_of(block * block_rows, block_rows), block_rows), :]
        return values.reshape(INNER, ROWS, LANES)

    def receive(step):
        @pl.when(step == 0)
        def _():
            own_chunk.wait()
            own_place.wait()
            awaited(
                send_ref.at[pl.ds(0, block_rows - ROWS)],
                recv_ref.at[pl.ds(0, block_rows - ROWS)],
                send_sems.at[0],
                recv_sems.at[0],
            ).wait_recv()

        @pl.when(step > 0)
        def _():
            awaited(
                send_ref.at[pl.ds(0, block_rows)],
                recv_ref.at[pl.ds(0, block_rows)],
                send_sems.at[0],
                recv_sems.at[step],
            ).wait_recv()
            awaited(place_ref, places_ref.at[0], send_sems.at[1], place_sems.at[step]).wait_recv()

        values = block_values(block_of(step))
        for parity in range(2):
            value = values[:, parity * 2 * SEGMENTS : (parity + 1) * 2 * SEGMENTS, :].reshape(LANES, LANES)
            high, low = split(value)
            stacked = jnp.concatenate([high, low, high], 0)

            def place_at(slot):
                right_ref[parity, :, pl.ds(pl.multiple_of(slot * LANES, LANES), LANES)] = stacked

            place_at(BLOCKS + 1 - step)

            @pl.when(step < 2)
            def _():
                place_at(1 - step)

            @pl.when(step >= BLOCKS - 2)
            def _():
                place_at(BLOCKS + 1 - step + BLOCKS)

    def correlate(step):
        block = block_of(step)
        values = block_values(block)
        place = jnp.concatenate([places_ref[block], jnp.zeros((LANES - 4 * PAIRS, LANES), jnp.int32)], 0).T
        lane = place % LANES
        code = place // LANES * 4 + lanes % 4
        picked = jnp.zeros((LANES, LANES), jnp.float32)
        columns = pl.ds(pl.multiple_of((BLOCKS - 1 - step) * LANES, LANES), SPAN * LANES)
        for parity in range(2):
            value = values[:, parity * 2 * SEGMENTS : (parity + 1) * 2 * SEGMENTS, :]
            turned = pltpu.roll(value, SEGMENTS, 1)
            turned = jnp.where(flips, turned, -turned)
            left = jnp.concatenate([value.reshape(LANES, LANES).T, turned.reshape(LANES, LANES).T], 0)
            high, low = split(left)
            gram = dot(jnp.concatenate([high, high, low], 1), right_ref[parity, :, columns], ((1,), (0,)))
            for component in range(2):
                for near in range(SPAN):
                    tile = gram[
                        component * LANES : (component + 1) * LANES, near * LANES : (near + 1) * LANES
                    ]
                    value_there = jnp.take_along_axis(tile, lane, axis=1, mode="promise_in_bounds")
                    picked = jnp.where(code == near * 4 + parity * 2 + component, value_there, picked)
        picked = picked.T
        for pair in range(PAIRS):
            found_ref[step, pair] = picked[4 * pair : 4 * pair + 4]

        def send_pair(shift, _):
            pair = lax.rem(my_inner + shift, INNER)
            pltpu.make_async_remote_copy(
                src_ref=found_ref.at[step, pair],
                dst_ref=cross_ref.at[me],
                send_sem=send_sems.at[2],
                recv_sem=cross_sem,
                device_id=(block, pair),
                device_id_type=MESH,
            ).start()
            return 0

        lax.fori_loop(1, INNER, send_pair, 0)

        @pl.when(step > 0)
        def _():
            send_pair(0, 0)

    def first_sends(step, _):
        send_step(step)
        return 0

    lax.fori_loop(0, AHEAD, first_sends, 0)

    def round_trip(turn, _):
        @pl.when(turn < BLOCKS - AHEAD)
        def _():
            send_step(turn + AHEAD)

        @pl.when(turn < BLOCKS)
        def _():
            receive(turn)

        @pl.when(turn >= 2 * REACH)
        def _():
            correlate(lax.rem(turn - REACH, BLOCKS))

        return 0

    lax.fori_loop(0, BLOCKS + 2 * REACH, round_trip, 0)

    own_cross = pltpu.make_async_copy(found_ref.at[0, my_inner], cross_ref.at[me], local_sems.at[2])
    own_cross.start()
    own_cross.wait()
    awaited(
        cross_ref.at[pl.ds(0, DEVICES - 1)], cross_ref.at[pl.ds(0, DEVICES - 1)], send_sems.at[2], cross_sem
    ).wait_recv()

    sums = []
    for parity in range(2):
        total = None
        for component in range(2):
            place = parity * 2 + component
            high, low = split(cross_ref[:, place, :])
            rows = table_ref[pl.ds(place * QUARTER, QUARTER), :]
            table_high, table_low = rows[:, :half], rows[:, 2 * half :]
            first = ((0,), (0,))
            term = dot(high, table_high, first) + (dot(high, table_low, first) + dot(low, table_high, first))
            total = term if total is None else total + term
        sums.append(total)
    even, odd = sums
    shift = LAGS // 2
    segment_count = INNER * SEGMENTS
    factor = math.sqrt(segment_count / F) / segment_count
    out_ref[0, :, pl.ds(0, shift)] = (even - odd)[:, half - shift :] * factor
    out_ref[0, :, pl.ds(shift, shift)] = (even + odd)[:, :shift] * factor

    rest = DEVICES * ROWS - ROWS
    awaited(send_ref.at[pl.ds(0, rest)], recv_ref.at[pl.ds(0, rest)], send_sems.at[0], recv_sems.at[0]).wait_send()
    awaited(
        places_ref.at[pl.ds(0, BLOCKS - 1)], places_ref.at[pl.ds(0, BLOCKS - 1)], send_sems.at[1], place_sems.at[0]
    ).wait_send()
    awaited(
        cross_ref.at[pl.ds(0, DEVICES - 1)], cross_ref.at[pl.ds(0, DEVICES - 1)], send_sems.at[2], cross_sem
    ).wait_send()


def local(records, starts, offsets):
    high, low = split_table()
    vmem = pl.BlockSpec(memory_space=pltpu.VMEM)
    hbm = pl.BlockSpec(memory_space=pltpu.HBM)
    dma = pltpu.SemaphoreType.DMA
    pieces = pl.pallas_call(
        cut_kernel,
        out_shape=jax.ShapeDtypeStruct((SEGMENTS, LANES, SEG), jnp.float32),
        in_specs=[hbm, hbm],
        out_specs=vmem,
        scratch_shapes=[
            pltpu.SMEM((SEGMENTS,), jnp.int32),
            pltpu.VMEM((SEGMENTS, LANES, CUT), jnp.float32),
            dma,
            dma((SEGMENTS,)),
        ],
        compiler_params=pltpu.CompilerParams(vmem_limit_bytes=56 << 20),
    )(starts, records)
    return pl.pallas_call(
        kernel,
        out_shape=jax.ShapeDtypeStruct((1, LANES, LAGS), jnp.float32),
        in_specs=[hbm, vmem, hbm, hbm],
        out_specs=vmem,
        scratch_shapes=[
            pltpu.VMEM((PAIRS, LANES), jnp.int32),
            pltpu.VMEM((2 * F, 3 * (SEG // 2)), jnp.bfloat16),
            pltpu.VMEM((F, 2 * F), jnp.bfloat16),
            pltpu.VMEM((DEVICES * ROWS, LANES), jnp.float32),
            pltpu.VMEM((DEVICES * ROWS, LANES), jnp.float32),
            pltpu.VMEM((4 * PAIRS, LANES), jnp.int32),
            pltpu.VMEM((BLOCKS, 4 * PAIRS, LANES), jnp.int32),
            pltpu.VMEM((2, 3 * LANES, (BLOCKS + 2 * REACH) * LANES), jnp.bfloat16),
            pltpu.VMEM((BLOCKS, PAIRS, 4, LANES), jnp.float32),
            pltpu.VMEM((DEVICES, 4, LANES), jnp.float32),
            dma,
            dma((3,)),
            dma((3,)),
            dma((3,)),
            dma((BLOCKS,)),
            dma((BLOCKS,)),
            dma,
        ],
        compiler_params=pltpu.CompilerParams(
            collective_id=0, has_side_effects=True, vmem_limit_bytes=58 << 20
        ),
    )(offsets.T, pieces, jnp.asarray(high), jnp.asarray(low))


def solution(mesh):
    placed = (P("blk", "inner", None), P("inner"), P("blk", None))
    return jax.shard_map(
        local, mesh=mesh, in_specs=placed, out_specs=P("inner", "blk", None), check_vma=False
    )
```

```python
import math

import ml_dtypes
import numpy as np

import jax
import jax.numpy as jnp
from jax import lax
from jax.experimental import pallas as pl
from jax.experimental.pallas import tpu as pltpu
from jax.sharding import PartitionSpec as P

SEG = 1024
SLOT = 2048
LAGS = 768
HALF = 32
PAIRS = 16
F = 512
SEP = 256
LANES = 128
CUT = SEG + LANES
BLOCKS = 16
INNER = 16
DEVICES = BLOCKS * INNER
SEGMENTS = 4
ROWS = 4 * SEGMENTS
QUARTER = F // 2
REACH = SEP // LANES
SPAN = 2 * REACH + 1
MESH = pl.DeviceIdType.MESH


def split_table():
    samples = np.arange(SEG // 2, dtype=np.int64)
    rows = []
    for parity in range(2):
        bins = 2 * np.arange(QUARTER, dtype=np.int64) + parity
        angle = 2.0 * np.pi / SEG * (bins[:, None] * samples[None, :] % SEG)
        rows += [np.cos(angle), -np.sin(angle)]
    table = np.concatenate(rows, 0).astype(np.float32)
    high = table.astype(ml_dtypes.bfloat16)
    low = (table - high.astype(np.float32)).astype(ml_dtypes.bfloat16)
    return high, low


def split(value):
    high = value.astype(jnp.bfloat16)
    low = (value - high.astype(jnp.float32)).astype(jnp.bfloat16)
    return high, low


def dot(left, right, dims):
    return lax.dot_general(left, right, (dims, ((), ())), preferred_element_type=jnp.float32)


def kernel(
    starts_hbm,
    offsets_hbm,
    records_ref,
    high_ref,
    low_ref,
    out_ref,
    starts_ref,
    offsets_ref,
    slots_ref,
    table_ref,
    band_ref,
    send_ref,
    recv_ref,
    place_ref,
    places_ref,
    right_ref,
    found_ref,
    cross_ref,
    index_sems,
    load_sems,
    table_sems,
    local_sems,
    send_sems,
    recv_sems,
    place_sems,
    cross_sem,
    row_sem,
):
    my_block = lax.axis_index("blk")
    my_inner = lax.axis_index("inner")
    me = my_block * INNER + my_inner
    half = SEG // 2

    def load_table(part):
        source = (high_ref, high_ref, low_ref)[part]
        return pltpu.make_async_copy(source, table_ref.at[:, pl.ds(part * half, half)], table_sems.at[part])

    def load_segment(segment):
        return pltpu.make_async_copy(records_ref.at[:, segment, :], slots_ref.at[segment], load_sems.at[segment])

    load_starts = pltpu.make_async_copy(starts_hbm, starts_ref, index_sems.at[0])
    load_offsets = pltpu.make_async_copy(offsets_hbm, offsets_ref, index_sems.at[1])
    load_starts.start()
    load_offsets.start()
    for segment in range(2):
        load_segment(segment).start()
    for part in range(3):
        load_table(part).start()
    for segment in range(2, SEGMENTS):
        load_segment(segment).start()

    barrier = pltpu.get_barrier_semaphore()

    def peer_in_row(step):
        return (my_block, (my_inner + step) & (INNER - 1))

    def peer_in_column(step):
        return ((my_block + step) & (BLOCKS - 1), my_inner)

    def greet(step, _):
        pl.semaphore_signal(barrier, inc=1, device_id=peer_in_row(step), device_id_type=MESH)
        pl.semaphore_signal(barrier, inc=1, device_id=peer_in_column(step), device_id_type=MESH)
        return 0

    lax.fori_loop(1, INNER, greet, 0)

    load_offsets.wait()
    channel_ids = lax.broadcasted_iota(jnp.int32, (1, LANES), 1)
    for pair in range(PAIRS):
        row = offsets_ref[pl.ds(pair, 1), :] + (channel_ids + SEP)
        place_ref[pl.ds(4 * pair, 4), :] = jnp.broadcast_to(row, (4, LANES))

    gap = 2 * (
        lax.broadcasted_iota(jnp.int32, (QUARTER, QUARTER), 0) - lax.broadcasted_iota(jnp.int32, (QUARTER, QUARTER), 1)
    )

    def near_bins(shift):
        distance = jnp.abs(gap + shift)
        distance = jnp.minimum(distance, F - distance)
        return jnp.where(distance <= HALF, 1.0, 0.0).astype(jnp.bfloat16)

    same, after, before = near_bins(0), near_bins(1), near_bins(-1)
    for copy in range(2):
        band_ref[pl.ds(0, QUARTER), pl.ds(copy * F, QUARTER)] = same
        band_ref[pl.ds(0, QUARTER), pl.ds(copy * F + QUARTER, QUARTER)] = before
        band_ref[pl.ds(QUARTER, QUARTER), pl.ds(copy * F, QUARTER)] = after
        band_ref[pl.ds(QUARTER, QUARTER), pl.ds(copy * F + QUARTER, QUARTER)] = same
    samples = lax.broadcasted_iota(jnp.int32, (8, SEG), 1).astype(jnp.float32)
    window = (0.5 - 0.5 * jnp.cos(2.0 * jnp.pi / SEG * samples))[:1]
    load_starts.wait()
    lanes = lax.broadcasted_iota(jnp.int32, (LANES, LANES), 1)
    for part in range(3):
        load_table(part).wait()

    def transform(first_segment):
        pieces = []
        for segment in range(first_segment, first_segment + 2):
            load_segment(segment).wait()
            begin = jnp.full((LANES, LANES), starts_ref[segment], jnp.int32)
            first = jnp.minimum(begin >> 7, (SLOT - CUT) // LANES)
            tiles = [slots_ref[segment, :, pl.ds(at, LANES)] for at in range(0, SLOT, LANES)]
            for bit, kept in ((4, CUT // LANES + 3), (2, CUT // LANES + 1), (1, CUT // LANES)):
                moved = (first & bit) != 0
                tiles = [jnp.where(moved, tiles[at + bit], tiles[at]) for at in range(kept)]
            place = lanes + (begin - first * LANES)
            stays = place < LANES
            place = place & (LANES - 1)
            turned = [jnp.take_along_axis(tile, place, axis=1, mode="promise_in_bounds") for tile in tiles]
            piece = [jnp.where(stays, turned[at], turned[at + 1]) for at in range(SEG // LANES)]
            pieces.append(jnp.concatenate(piece, 1) * window)
        piece = jnp.concatenate(pieces, 0)
        parts = []
        for parity in range(2):
            front, back = piece[:, :half], piece[:, half:]
            high, low = split(front + back if parity == 0 else front - back)
            stacked = jnp.concatenate([high, low, high], 1)
            rows = table_ref[pl.ds(parity * 2 * QUARTER, 2 * QUARTER), :]
            parts.append(dot(rows, stacked, ((1,), (1,))))
        power = jnp.concatenate(
            [part[:QUARTER] * part[:QUARTER] + part[QUARTER:] * part[QUARTER:] for part in parts], 0
        )
        smooth = dot(band_ref[...], jnp.concatenate(split(power), 0), ((1,), (0,)))
        scale = lax.rsqrt(smooth * (1.0 / (2 * HALF + 1)) + 1e-06)
        for parity in range(2):
            part_scale = scale[parity * QUARTER : (parity + 1) * QUARTER]
            for component in range(2):
                value = parts[parity][component * QUARTER : (component + 1) * QUARTER] * part_scale
                for second in range(2):
                    row = (parity * 2 + component) * SEGMENTS + first_segment + second
                    send_ref[pl.ds(row, QUARTER, stride=ROWS), :] = value[:, second * LANES : (second + 1) * LANES]

    transform(0)
    pl.semaphore_wait(barrier, 2 * (INNER - 1))

    def pass_on(step, _):
        pl.semaphore_signal(row_sem, inc=1, device_id=peer_in_column(step), device_id_type=MESH)
        return 0

    lax.fori_loop(1, BLOCKS, pass_on, 0)
    transform(2)
    pl.semaphore_wait(row_sem, BLOCKS - 1)

    def chunk(device):
        return pl.ds(pl.multiple_of(device * ROWS, ROWS), ROWS)

    own_chunk = pltpu.make_async_copy(send_ref.at[chunk(me)], recv_ref.at[chunk(me)], local_sems.at[0])
    own_chunk.start()
    own_place = pltpu.make_async_copy(place_ref, places_ref.at[my_block], local_sems.at[1])
    own_place.start()

    def send_step(step):
        block = lax.rem(my_block + step, BLOCKS)

        def send_one(shift, _):
            other = lax.rem(my_inner + shift, INNER)
            pltpu.make_async_remote_copy(
                src_ref=send_ref.at[chunk(block * INNER + other)],
                dst_ref=recv_ref.at[chunk(me)],
                send_sem=send_sems.at[0],
                recv_sem=recv_sems.at[step],
                device_id=(block, other),
                device_id_type=MESH,
            ).start()
            return 0

        lax.fori_loop(1, INNER, send_one, 0)

        @pl.when(step > 0)
        def _():
            send_one(0, 0)
            pltpu.make_async_remote_copy(
                src_ref=place_ref,
                dst_ref=places_ref.at[my_block],
                send_sem=send_sems.at[1],
                recv_sem=place_sems.at[step],
                device_id=(block, my_inner),
                device_id_type=MESH,
            ).start()

    next_device = (lax.rem(my_block + 1, BLOCKS), my_inner)

    def awaited(source, target, send_sem, recv_sem):
        return pltpu.make_async_remote_copy(
            src_ref=source,
            dst_ref=target,
            send_sem=send_sem,
            recv_sem=recv_sem,
            device_id=next_device,
            device_id_type=MESH,
        )

    block_rows = INNER * ROWS
    flips = lax.broadcasted_iota(jnp.int32, (INNER, 2 * SEGMENTS, LANES), 1) < SEGMENTS

    def block_of(step):
        return lax.rem(my_block + BLOCKS - step, BLOCKS)

    def block_values(block):
        values = recv_ref[pl.ds(pl.multiple_of(block * block_rows, block_rows), block_rows), :]
        return values.reshape(INNER, ROWS, LANES)

    def receive(step):
        @pl.when(step == 0)
        def _():
            own_chunk.wait()
            own_place.wait()
            awaited(
                send_ref.at[pl.ds(0, block_rows - ROWS)],
                recv_ref.at[pl.ds(0, block_rows - ROWS)],
                send_sems.at[0],
                recv_sems.at[0],
            ).wait_recv()

        @pl.when(step > 0)
        def _():
            awaited(
                send_ref.at[pl.ds(0, block_rows)],
                recv_ref.at[pl.ds(0, block_rows)],
                send_sems.at[0],
                recv_sems.at[step],
            ).wait_recv()
            awaited(place_ref, places_ref.at[0], send_sems.at[1], place_sems.at[step]).wait_recv()

        values = block_values(block_of(step))
        for parity in range(2):
            value = values[:, parity * 2 * SEGMENTS : (parity + 1) * 2 * SEGMENTS, :].reshape(LANES, LANES)
            high, low = split(value)
            stacked = jnp.concatenate([high, low, high], 0)

            def place_at(slot):
                right_ref[parity, :, pl.ds(pl.multiple_of(slot * LANES, LANES), LANES)] = stacked

            place_at(BLOCKS + 1 - step)

            @pl.when(step < 2)
            def _():
                place_at(1 - step)

            @pl.when(step >= BLOCKS - 2)
            def _():
                place_at(BLOCKS + 1 - step + BLOCKS)

    def correlate(step):
        block = block_of(step)
        values = block_values(block)
        place = jnp.concatenate([places_ref[block], jnp.zeros((LANES - 4 * PAIRS, LANES), jnp.int32)], 0).T
        lane = place % LANES
        code = place // LANES * 4 + lanes % 4
        picked = jnp.zeros((LANES, LANES), jnp.float32)
        columns = pl.ds(pl.multiple_of((BLOCKS - 1 - step) * LANES, LANES), SPAN * LANES)
        for parity in range(2):
            value = values[:, parity * 2 * SEGMENTS : (parity + 1) * 2 * SEGMENTS, :]
            turned = pltpu.roll(value, SEGMENTS, 1)
            turned = jnp.where(flips, turned, -turned)
            left = jnp.concatenate([value.reshape(LANES, LANES).T, turned.reshape(LANES, LANES).T], 0)
            high, low = split(left)
            gram = dot(jnp.concatenate([high, high, low], 1), right_ref[parity, :, columns], ((1,), (0,)))
            for component in range(2):
                for near in range(SPAN):
                    tile = gram[
                        component * LANES : (component + 1) * LANES, near * LANES : (near + 1) * LANES
                    ]
                    value_there = jnp.take_along_axis(tile, lane, axis=1, mode="promise_in_bounds")
                    picked = jnp.where(code == near * 4 + parity * 2 + component, value_there, picked)
        picked = picked.T
        for pair in range(PAIRS):
            found_ref[step, pair] = picked[4 * pair : 4 * pair + 4]

        def send_pair(shift, _):
            pair = lax.rem(my_inner + shift, INNER)
            pltpu.make_async_remote_copy(
                src_ref=found_ref.at[step, pair],
                dst_ref=cross_ref.at[me],
                send_sem=send_sems.at[2],
                recv_sem=cross_sem,
                device_id=(block, pair),
                device_id_type=MESH,
            ).start()
            return 0

        lax.fori_loop(1, INNER, send_pair, 0)

        @pl.when(step > 0)
        def _():
            send_pair(0, 0)

    def all_sends(step, _):
        send_step(step)
        return 0

    lax.fori_loop(0, BLOCKS, all_sends, 0)

    def round_trip(turn, _):
        @pl.when(turn < BLOCKS)
        def _():
            receive(turn)

        @pl.when(turn >= 2 * REACH)
        def _():
            correlate(lax.rem(turn - REACH, BLOCKS))

        return 0

    lax.fori_loop(0, BLOCKS + 2 * REACH, round_trip, 0)

    own_cross = pltpu.make_async_copy(found_ref.at[0, my_inner], cross_ref.at[me], local_sems.at[2])
    own_cross.start()
    own_cross.wait()
    awaited(
        cross_ref.at[pl.ds(0, DEVICES - 1)], cross_ref.at[pl.ds(0, DEVICES - 1)], send_sems.at[2], cross_sem
    ).wait_recv()

    sums = []
    for parity in range(2):
        total = None
        for component in range(2):
            place = parity * 2 + component
            high, low = split(cross_ref[:, place, :])
            rows = table_ref[pl.ds(place * QUARTER, QUARTER), :]
            table_high, table_low = rows[:, :half], rows[:, 2 * half :]
            first = ((0,), (0,))
            term = dot(high, table_high, first) + (dot(high, table_low, first) + dot(low, table_high, first))
            total = term if total is None else total + term
        sums.append(total)
    even, odd = sums
    shift = LAGS // 2
    segment_count = INNER * SEGMENTS
    factor = math.sqrt(segment_count / F) / segment_count
    out_ref[0, :, pl.ds(0, shift)] = (even - odd)[:, half - shift :] * factor
    out_ref[0, :, pl.ds(shift, shift)] = (even + odd)[:, :shift] * factor

    rest = DEVICES * ROWS - ROWS
    awaited(send_ref.at[pl.ds(0, rest)], recv_ref.at[pl.ds(0, rest)], send_sems.at[0], recv_sems.at[0]).wait_send()
    awaited(
        places_ref.at[pl.ds(0, BLOCKS - 1)], places_ref.at[pl.ds(0, BLOCKS - 1)], send_sems.at[1], place_sems.at[0]
    ).wait_send()
    awaited(
        cross_ref.at[pl.ds(0, DEVICES - 1)], cross_ref.at[pl.ds(0, DEVICES - 1)], send_sems.at[2], cross_sem
    ).wait_send()


def local(records, starts, offsets):
    high, low = split_table()
    vmem = pl.BlockSpec(memory_space=pltpu.VMEM)
    hbm = pl.BlockSpec(memory_space=pltpu.HBM)
    dma = pltpu.SemaphoreType.DMA
    return pl.pallas_call(
        kernel,
        out_shape=jax.ShapeDtypeStruct((1, LANES, LAGS), jnp.float32),
        in_specs=[hbm] * 5,
        out_specs=vmem,
        scratch_shapes=[
            pltpu.SMEM((SEGMENTS,), jnp.int32),
            pltpu.VMEM((PAIRS, LANES), jnp.int32),
            pltpu.VMEM((SEGMENTS, LANES, SLOT), jnp.float32),
            pltpu.VMEM((2 * F, 3 * (SEG // 2)), jnp.bfloat16),
            pltpu.VMEM((F, 2 * F), jnp.bfloat16),
            pltpu.VMEM((DEVICES * ROWS, LANES), jnp.float32),
            pltpu.VMEM((DEVICES * ROWS, LANES), jnp.float32),
            pltpu.VMEM((4 * PAIRS, LANES), jnp.int32),
            pltpu.VMEM((BLOCKS, 4 * PAIRS, LANES), jnp.int32),
            pltpu.VMEM((2, 3 * LANES, (BLOCKS + 2 * REACH) * LANES), jnp.bfloat16),
            pltpu.VMEM((BLOCKS, PAIRS, 4, LANES), jnp.float32),
            pltpu.VMEM((DEVICES, 4, LANES), jnp.float32),
            dma((2,)),
            dma((SEGMENTS,)),
            dma((3,)),
            dma((3,)),
            dma((3,)),
            dma((BLOCKS,)),
            dma((BLOCKS,)),
            dma,
            pltpu.SemaphoreType.REGULAR,
        ],
        compiler_params=pltpu.CompilerParams(
            collective_id=0, has_side_effects=True, vmem_limit_bytes=58 << 20
        ),
    )(starts, offsets.T, records, jnp.asarray(high), jnp.asarray(low))


def solution(mesh):
    placed = (P("blk", "inner", None), P("inner"), P("blk", None))
    return jax.shard_map(
        local, mesh=mesh, in_specs=placed, out_specs=P("inner", "blk", None), check_vma=False
    )
```

```python
import math

import ml_dtypes
import numpy as np

import jax
import jax.numpy as jnp
from jax import lax
from jax.experimental import pallas as pl
from jax.experimental.pallas import tpu as pltpu
from jax.sharding import PartitionSpec as P

SEG = 1024
SLOT = 2048
LAGS = 768
HALF = 32
PAIRS = 16
F = 512
SEP = 256
LANES = 128
CUT = SEG + LANES
BLOCKS = 16
INNER = 16
DEVICES = BLOCKS * INNER
SEGMENTS = 4
ROWS = 4 * SEGMENTS
HALF_ROWS = ROWS // 2
HEAD = 4
QUARTER = F // 2
REACH = SEP // LANES
SPAN = 2 * REACH + 1
MESH = pl.DeviceIdType.MESH


def split_table():
    samples = np.arange(SEG // 2, dtype=np.int64)
    rows = []
    for parity in range(2):
        bins = 2 * np.arange(QUARTER, dtype=np.int64) + parity
        angle = 2.0 * np.pi / SEG * (bins[:, None] * samples[None, :] % SEG)
        rows += [np.cos(angle), -np.sin(angle)]
    table = np.concatenate(rows, 0).astype(np.float32)
    high = table.astype(ml_dtypes.bfloat16)
    low = (table - high.astype(np.float32)).astype(ml_dtypes.bfloat16)
    return high, low


def split(value):
    high = value.astype(jnp.bfloat16)
    low = (value - high.astype(jnp.float32)).astype(jnp.bfloat16)
    return high, low


def dot(left, right, dims):
    return lax.dot_general(left, right, (dims, ((), ())), preferred_element_type=jnp.float32)


def kernel(
    starts_hbm,
    offsets_hbm,
    records_ref,
    high_ref,
    low_ref,
    out_ref,
    starts_ref,
    offsets_ref,
    slots_ref,
    table_ref,
    band_ref,
    send_ref,
    recv_ref,
    place_ref,
    places_ref,
    right_ref,
    found_ref,
    cross_ref,
    index_sems,
    load_sems,
    table_sems,
    local_sems,
    send_sems,
    recv_sems,
    place_sems,
    cross_sem,
    row_sem,
):
    my_block = lax.axis_index("blk")
    my_inner = lax.axis_index("inner")
    me = my_block * INNER + my_inner
    half = SEG // 2

    def load_table(part):
        source = (high_ref, low_ref)[part]
        return pltpu.make_async_copy(source, table_ref.at[:, pl.ds(part * half, half)], table_sems.at[part])

    def load_segment(segment):
        return pltpu.make_async_copy(records_ref.at[:, segment, :], slots_ref.at[segment], load_sems.at[segment])

    load_starts = pltpu.make_async_copy(starts_hbm, starts_ref, index_sems.at[0])
    load_offsets = pltpu.make_async_copy(offsets_hbm, offsets_ref, index_sems.at[1])
    load_starts.start()
    load_offsets.start()
    for segment in range(2):
        load_segment(segment).start()
    for part in range(2):
        load_table(part).start()
    for segment in range(2, SEGMENTS):
        load_segment(segment).start()

    barrier = pltpu.get_barrier_semaphore()

    def peer_in_row(step):
        return (my_block, (my_inner + step) & (INNER - 1))

    def peer_in_column(step):
        return ((my_block + step) & (BLOCKS - 1), my_inner)

    def greet(step, _):
        pl.semaphore_signal(barrier, inc=1, device_id=peer_in_row(step), device_id_type=MESH)
        pl.semaphore_signal(barrier, inc=1, device_id=peer_in_column(step), device_id_type=MESH)
        return 0

    lax.fori_loop(1, INNER, greet, 0)

    pl.semaphore_wait(barrier, 2 * (INNER - 1))

    def pass_on(step, _):
        pl.semaphore_signal(row_sem, inc=1, device_id=peer_in_column(step), device_id_type=MESH)
        return 0

    lax.fori_loop(1, BLOCKS, pass_on, 0)

    load_offsets.wait()
    channel_ids = lax.broadcasted_iota(jnp.int32, (1, LANES), 1)
    for pair in range(PAIRS):
        row = offsets_ref[pl.ds(pair, 1), :] + (channel_ids + SEP)
        place_ref[pl.ds(4 * pair, 4), :] = jnp.broadcast_to(row, (4, LANES))

    gap = 2 * (
        lax.broadcasted_iota(jnp.int32, (QUARTER, QUARTER), 0) - lax.broadcasted_iota(jnp.int32, (QUARTER, QUARTER), 1)
    )

    def near_bins(shift):
        distance = jnp.abs(gap + shift)
        distance = jnp.minimum(distance, F - distance)
        return jnp.where(distance <= HALF, 1.0, 0.0).astype(jnp.bfloat16)

    same, after, before = near_bins(0), near_bins(1), near_bins(-1)
    for copy in range(2):
        band_ref[pl.ds(0, QUARTER), pl.ds(copy * F, QUARTER)] = same
        band_ref[pl.ds(0, QUARTER), pl.ds(copy * F + QUARTER, QUARTER)] = before
        band_ref[pl.ds(QUARTER, QUARTER), pl.ds(copy * F, QUARTER)] = after
        band_ref[pl.ds(QUARTER, QUARTER), pl.ds(copy * F + QUARTER, QUARTER)] = same
    samples = lax.broadcasted_iota(jnp.int32, (8, SEG), 1).astype(jnp.float32)
    window = (0.5 - 0.5 * jnp.cos(2.0 * jnp.pi / SEG * samples))[:1]
    load_starts.wait()
    lanes = lax.broadcasted_iota(jnp.int32, (LANES, LANES), 1)
    for part in range(2):
        load_table(part).wait()

    def transform(first_segment):
        pieces = []
        for segment in range(first_segment, first_segment + 2):
            load_segment(segment).wait()
            begin = jnp.full((LANES, LANES), starts_ref[segment], jnp.int32)
            first = jnp.minimum(begin >> 7, (SLOT - CUT) // LANES)
            tiles = [slots_ref[segment, :, pl.ds(at, LANES)] for at in range(0, SLOT, LANES)]
            for bit, kept in ((4, CUT // LANES + 3), (2, CUT // LANES + 1), (1, CUT // LANES)):
                moved = (first & bit) != 0
                tiles = [jnp.where(moved, tiles[at + bit], tiles[at]) for at in range(kept)]
            place = lanes + (begin - first * LANES)
            stays = place < LANES
            place = place & (LANES - 1)
            turned = [jnp.take_along_axis(tile, place, axis=1, mode="promise_in_bounds") for tile in tiles]
            piece = [jnp.where(stays, turned[at], turned[at + 1]) for at in range(SEG // LANES)]
            pieces.append(jnp.concatenate(piece, 1) * window)
        piece = jnp.concatenate(pieces, 0)
        parts = []
        for parity in range(2):
            front, back = piece[:, :half], piece[:, half:]
            high, low = split(front + back if parity == 0 else front - back)
            stacked = jnp.concatenate([high, low, high], 1)
            rows = table_ref[pl.ds(parity * 2 * QUARTER, 2 * QUARTER), :]
            rows = jnp.concatenate([rows[:, :half], rows], 1)
            parts.append(dot(rows, stacked, ((1,), (1,))))
        power = jnp.concatenate(
            [part[:QUARTER] * part[:QUARTER] + part[QUARTER:] * part[QUARTER:] for part in parts], 0
        )
        smooth = dot(band_ref[...], jnp.concatenate(split(power), 0), ((1,), (0,)))
        scale = lax.rsqrt(smooth * (1.0 / (2 * HALF + 1)) + 1e-06)
        for parity in range(2):
            part_scale = scale[parity * QUARTER : (parity + 1) * QUARTER]
            for component in range(2):
                value = parts[parity][component * QUARTER : (component + 1) * QUARTER] * part_scale
                for second in range(2):
                    row = first_segment // 2 * HALF_ROWS + (parity * 2 + component) * 2 + second
                    send_ref[pl.ds(row, QUARTER, stride=ROWS), :] = value[:, second * LANES : (second + 1) * LANES]

    transform(0)
    pl.semaphore_wait(row_sem, BLOCKS - 1)

    def chunk(device):
        return pl.ds(pl.multiple_of(device * ROWS, ROWS), ROWS)

    def part_of_chunk(device, first, count):
        return pl.ds(pl.multiple_of(device * ROWS + first, HALF_ROWS), count)

    def shift_of(place):
        away = (place + 1) >> 1
        return jnp.where((place & 1) == 1, away, INNER - away) & (INNER - 1)

    def send_step(step, first, count):
        block = (my_block + step) & (BLOCKS - 1)

        def send_one(place, _):
            other = (my_inner + shift_of(place)) & (INNER - 1)
            pltpu.make_async_remote_copy(
                src_ref=send_ref.at[part_of_chunk(block * INNER + other, first, count)],
                dst_ref=recv_ref.at[part_of_chunk(me, first, count)],
                send_sem=send_sems.at[0],
                recv_sem=recv_sems.at[step],
                device_id=(block, other),
                device_id_type=MESH,
            ).start()
            return 0

        lax.fori_loop(1, INNER, send_one, 0)

        @pl.when(step > 0)
        def _():
            send_one(0, 0)

    def send_places(step, _):
        pltpu.make_async_remote_copy(
            src_ref=place_ref,
            dst_ref=places_ref.at[my_block],
            send_sem=send_sems.at[1],
            recv_sem=place_sems.at[step],
            device_id=((my_block + step) & (BLOCKS - 1), my_inner),
            device_id_type=MESH,
        ).start()
        return 0

    def sends(first_step, last_step, first, count):
        def one_step(step, _):
            send_step(step, first, count)
            return 0

        lax.fori_loop(first_step, last_step, one_step, 0)

    own_place = pltpu.make_async_copy(place_ref, places_ref.at[my_block], local_sems.at[1])
    own_place.start()
    sends(0, HEAD, 0, HALF_ROWS)
    transform(2)
    own_chunk = pltpu.make_async_copy(send_ref.at[chunk(me)], recv_ref.at[chunk(me)], local_sems.at[0])
    own_chunk.start()
    sends(0, HEAD, HALF_ROWS, HALF_ROWS)
    lax.fori_loop(1, BLOCKS, send_places, 0)
    sends(HEAD, BLOCKS, 0, ROWS)

    next_device = (lax.rem(my_block + 1, BLOCKS), my_inner)

    def awaited(source, target, send_sem, recv_sem):
        return pltpu.make_async_remote_copy(
            src_ref=source,
            dst_ref=target,
            send_sem=send_sem,
            recv_sem=recv_sem,
            device_id=next_device,
            device_id_type=MESH,
        )

    block_rows = INNER * ROWS
    places8 = lax.broadcasted_iota(jnp.int32, (INNER, HALF_ROWS, LANES), 1)
    lower = places8 < HALF_ROWS // 2
    real = places8 & 2 == 0

    def block_of(step):
        return lax.rem(my_block + BLOCKS - step, BLOCKS)

    def block_values(block):
        values = recv_ref[pl.ds(pl.multiple_of(block * block_rows, block_rows), block_rows), :]
        values = values.reshape(INNER, ROWS, LANES)
        early, late = values[:, :HALF_ROWS], values[:, HALF_ROWS:]
        turn = HALF_ROWS // 2
        return (
            jnp.where(lower, early, pltpu.roll(late, turn, 1)),
            jnp.where(lower, pltpu.roll(early, turn, 1), late),
        )

    def receive(step):
        @pl.when(step == 0)
        def _():
            own_chunk.wait()
            own_place.wait()
            awaited(
                send_ref.at[pl.ds(0, block_rows - ROWS)],
                recv_ref.at[pl.ds(0, block_rows - ROWS)],
                send_sems.at[0],
                recv_sems.at[0],
            ).wait_recv()

        @pl.when(step > 0)
        def _():
            awaited(
                send_ref.at[pl.ds(0, block_rows)],
                recv_ref.at[pl.ds(0, block_rows)],
                send_sems.at[0],
                recv_sems.at[step],
            ).wait_recv()
            awaited(place_ref, places_ref.at[0], send_sems.at[1], place_sems.at[step]).wait_recv()

        values = block_values(block_of(step))
        for parity in range(2):
            value = values[parity].reshape(LANES, LANES)
            high, low = split(value)
            stacked = jnp.concatenate([high, low, high], 0)

            def place_at(slot):
                right_ref[parity, :, pl.ds(pl.multiple_of(slot * LANES, LANES), LANES)] = stacked

            place_at(BLOCKS + 1 - step)

            @pl.when(step < 2)
            def _():
                place_at(1 - step)

            @pl.when(step >= BLOCKS - 2)
            def _():
                place_at(BLOCKS + 1 - step + BLOCKS)

    def correlate(step):
        block = block_of(step)
        values = block_values(block)
        place = jnp.concatenate([places_ref[block], jnp.zeros((LANES - 4 * PAIRS, LANES), jnp.int32)], 0).T
        lane = place % LANES
        code = place // LANES * 4 + lanes % 4
        picked = jnp.zeros((LANES, LANES), jnp.float32)
        columns = pl.ds(pl.multiple_of((BLOCKS - 1 - step) * LANES, LANES), SPAN * LANES)
        for parity in range(2):
            value = values[parity]
            turned = jnp.where(real, pltpu.roll(value, HALF_ROWS - 2, 1), -pltpu.roll(value, 2, 1))
            left = jnp.concatenate([value.reshape(LANES, LANES).T, turned.reshape(LANES, LANES).T], 0)
            high, low = split(left)
            gram = dot(jnp.concatenate([high, high, low], 1), right_ref[parity, :, columns], ((1,), (0,)))
            for component in range(2):
                for near in range(SPAN):
                    tile = gram[
                        component * LANES : (component + 1) * LANES, near * LANES : (near + 1) * LANES
                    ]
                    value_there = jnp.take_along_axis(tile, lane, axis=1, mode="promise_in_bounds")
                    picked = jnp.where(code == near * 4 + parity * 2 + component, value_there, picked)
        picked = picked.T
        for pair in range(PAIRS):
            found_ref[step, pair] = picked[4 * pair : 4 * pair + 4]

        def send_pair(shift, _):
            pair = (my_inner + shift_of(shift)) & (INNER - 1)
            pltpu.make_async_remote_copy(
                src_ref=found_ref.at[step, pair],
                dst_ref=cross_ref.at[me],
                send_sem=send_sems.at[2],
                recv_sem=cross_sem,
                device_id=(block, pair),
                device_id_type=MESH,
            ).start()
            return 0

        lax.fori_loop(1, INNER, send_pair, 0)

        @pl.when(step > 0)
        def _():
            send_pair(0, 0)

    def round_trip(turn, _):
        @pl.when(turn < BLOCKS)
        def _():
            receive(turn)

        @pl.when(turn >= 2 * REACH)
        def _():
            correlate(lax.rem(turn - REACH, BLOCKS))

        return 0

    lax.fori_loop(0, BLOCKS + 2 * REACH, round_trip, 0)

    own_cross = pltpu.make_async_copy(found_ref.at[0, my_inner], cross_ref.at[me], local_sems.at[2])
    own_cross.start()
    own_cross.wait()
    awaited(
        cross_ref.at[pl.ds(0, DEVICES - 1)], cross_ref.at[pl.ds(0, DEVICES - 1)], send_sems.at[2], cross_sem
    ).wait_recv()

    sums = []
    for parity in range(2):
        total = None
        for component in range(2):
            place = parity * 2 + component
            high, low = split(cross_ref[:, place, :])
            rows = table_ref[pl.ds(place * QUARTER, QUARTER), :]
            table_high, table_low = rows[:, :half], rows[:, half:]
            first = ((0,), (0,))
            term = dot(high, table_high, first) + (dot(high, table_low, first) + dot(low, table_high, first))
            total = term if total is None else total + term
        sums.append(total)
    even, odd = sums
    shift = LAGS // 2
    segment_count = INNER * SEGMENTS
    factor = math.sqrt(segment_count / F) / segment_count
    out_ref[0, :, pl.ds(0, shift)] = (even - odd)[:, half - shift :] * factor
    out_ref[0, :, pl.ds(shift, shift)] = (even + odd)[:, :shift] * factor

    rest = DEVICES * ROWS - ROWS
    awaited(send_ref.at[pl.ds(0, rest)], recv_ref.at[pl.ds(0, rest)], send_sems.at[0], recv_sems.at[0]).wait_send()
    awaited(
        places_ref.at[pl.ds(0, BLOCKS - 1)], places_ref.at[pl.ds(0, BLOCKS - 1)], send_sems.at[1], place_sems.at[0]
    ).wait_send()
    awaited(
        cross_ref.at[pl.ds(0, DEVICES - 1)], cross_ref.at[pl.ds(0, DEVICES - 1)], send_sems.at[2], cross_sem
    ).wait_send()


def local(records, starts, offsets):
    high, low = split_table()
    vmem = pl.BlockSpec(memory_space=pltpu.VMEM)
    hbm = pl.BlockSpec(memory_space=pltpu.HBM)
    dma = pltpu.SemaphoreType.DMA
    operands = (starts, offsets.T, records, jnp.asarray(high), jnp.asarray(low))
    return pl.pallas_call(
        kernel,
        out_shape=jax.ShapeDtypeStruct((1, LANES, LAGS), jnp.float32),
        in_specs=[hbm] * 5,
        out_specs=vmem,
        scratch_shapes=[
            pltpu.SMEM((SEGMENTS,), jnp.int32),
            pltpu.VMEM((PAIRS, LANES), jnp.int32),
            pltpu.VMEM((SEGMENTS, LANES, SLOT), jnp.float32),
            pltpu.VMEM((2 * F, SEG), jnp.bfloat16),
            pltpu.VMEM((F, 2 * F), jnp.bfloat16),
            pltpu.VMEM((DEVICES * ROWS, LANES), jnp.float32),
            pltpu.VMEM((DEVICES * ROWS, LANES), jnp.float32),
            pltpu.VMEM((4 * PAIRS, LANES), jnp.int32),
            pltpu.VMEM((BLOCKS, 4 * PAIRS, LANES), jnp.int32),
            pltpu.VMEM((2, 3 * LANES, (BLOCKS + 2 * REACH) * LANES), jnp.bfloat16),
            pltpu.VMEM((BLOCKS, PAIRS, 4, LANES), jnp.float32),
            pltpu.VMEM((DEVICES, 4, LANES), jnp.float32),
            dma((2,)),
            dma((SEGMENTS,)),
            dma((2,)),
            dma((3,)),
            dma((3,)),
            dma((BLOCKS,)),
            dma((BLOCKS,)),
            dma,
            pltpu.SemaphoreType.REGULAR,
        ],
        compiler_params=pltpu.CompilerParams(
            collective_id=0, has_side_effects=True, vmem_limit_bytes=48 << 20
        ),
    )(*(pltpu.with_memory_space_constraint(value, pltpu.HBM) for value in operands))


def solution(mesh):
    placed = (P("blk", "inner", None), P("inner"), P("blk", None))
    return jax.shard_map(
        local, mesh=mesh, in_specs=placed, out_specs=P("inner", "blk", None), check_vma=False
    )
```

```python
import math

import ml_dtypes
import numpy as np

import jax
import jax.numpy as jnp
from jax import lax
from jax.experimental import pallas as pl
from jax.experimental.pallas import tpu as pltpu
from jax.sharding import PartitionSpec as P

SEG = 1024
SLOT = 2048
LAGS = 768
HALF = 32
PAIRS = 16
F = 512
SEP = 256
LANES = 128
CUT = SEG + LANES
BLOCKS = 16
INNER = 16
DEVICES = BLOCKS * INNER
SEGMENTS = 4
ROWS = 4 * SEGMENTS
PLANES = 8
OWNERS = DEVICES // 2
OWNED = 4
TILE = 2 * SEGMENTS
CHUNK = OWNED * TILE
BLOCK_ROWS = 8 * CHUNK
PARTS = 2 * OWNED
HEAD = 4
QUARTER = F // 2
REACH = SEP // LANES
SPAN = 2 * REACH + 1
MESH = pl.DeviceIdType.MESH


def split_table():
    samples = np.arange(SEG // 2, dtype=np.int64)
    rows = []
    for parity in range(2):
        order = np.arange(QUARTER, dtype=np.int64)
        bins = 2 * (order % OWNERS * 2 + order // OWNERS) + parity
        angle = 2.0 * np.pi / SEG * (bins[:, None] * samples[None, :] % SEG)
        rows += [np.cos(angle), -np.sin(angle)]
    table = np.concatenate(rows, 0).astype(np.float32)
    high = table.astype(ml_dtypes.bfloat16)
    low = (table - high.astype(np.float32)).astype(ml_dtypes.bfloat16)
    return high, low


def split(value):
    high = value.astype(jnp.bfloat16)
    low = (value - high.astype(jnp.float32)).astype(jnp.bfloat16)
    return high, low


def dot(left, right, dims):
    return lax.dot_general(left, right, (dims, ((), ())), preferred_element_type=jnp.float32)


def kernel(
    starts_hbm,
    offsets_hbm,
    records_ref,
    high_ref,
    low_ref,
    out_ref,
    starts_ref,
    offsets_ref,
    slots_ref,
    table_ref,
    band_ref,
    send_ref,
    recv_ref,
    places_ref,
    right_ref,
    found_ref,
    cross_ref,
    index_sems,
    load_sems,
    table_sems,
    local_sems,
    send_sems,
    recv_sems,
    place_sems,
    cross_sem,
    row_sem,
):
    my_block = lax.axis_index("blk")
    my_inner = lax.axis_index("inner")
    me = my_block * INNER + my_inner
    half = SEG // 2

    def load_table(part):
        source = (high_ref, low_ref)[part]
        return pltpu.make_async_copy(source, table_ref.at[:, pl.ds(part * half, half)], table_sems.at[part])

    def load_segment(segment):
        return pltpu.make_async_copy(records_ref.at[:, segment, :], slots_ref.at[segment], load_sems.at[segment])

    load_starts = pltpu.make_async_copy(starts_hbm, starts_ref, index_sems.at[0])
    load_offsets = pltpu.make_async_copy(offsets_hbm, offsets_ref, index_sems.at[1])
    load_starts.start()
    load_offsets.start()
    for segment in range(2):
        load_segment(segment).start()
    for part in range(2):
        load_table(part).start()
    for segment in range(2, SEGMENTS):
        load_segment(segment).start()

    barrier = pltpu.get_barrier_semaphore()

    def peer_in_row(step):
        return (my_block, (my_inner + step) & (INNER - 1))

    def peer_in_column(step):
        return ((my_block + step) & (BLOCKS - 1), my_inner)

    def greet(step, _):
        pl.semaphore_signal(barrier, inc=1, device_id=peer_in_row(step), device_id_type=MESH)
        pl.semaphore_signal(barrier, inc=1, device_id=peer_in_column(step), device_id_type=MESH)
        return 0

    lax.fori_loop(1, INNER, greet, 0)

    pl.semaphore_wait(barrier, 2 * (INNER - 1))

    def pass_on(step, _):
        pl.semaphore_signal(row_sem, inc=1, device_id=peer_in_column(step), device_id_type=MESH)
        return 0

    lax.fori_loop(1, BLOCKS, pass_on, 0)

    load_offsets.wait()
    def number(axis):
        order = lax.broadcasted_iota(jnp.int32, (QUARTER, QUARTER), axis)
        return ((order & (OWNERS - 1)) << 1) + (order >> 7)

    gap = 2 * (number(0) - number(1))

    def near_bins(shift):
        distance = jnp.abs(gap + shift)
        distance = jnp.minimum(distance, F - distance)
        return jnp.where(distance <= HALF, 1.0, 0.0).astype(jnp.bfloat16)

    same, after, before = near_bins(0), near_bins(1), near_bins(-1)
    for copy in range(2):
        band_ref[pl.ds(0, QUARTER), pl.ds(copy * F, QUARTER)] = same
        band_ref[pl.ds(0, QUARTER), pl.ds(copy * F + QUARTER, QUARTER)] = before
        band_ref[pl.ds(QUARTER, QUARTER), pl.ds(copy * F, QUARTER)] = after
        band_ref[pl.ds(QUARTER, QUARTER), pl.ds(copy * F + QUARTER, QUARTER)] = same
    samples = lax.broadcasted_iota(jnp.int32, (8, SEG), 1).astype(jnp.float32)
    window = (0.5 - 0.5 * jnp.cos(2.0 * jnp.pi / SEG * samples))[:1]
    load_starts.wait()
    lanes = lax.broadcasted_iota(jnp.int32, (LANES, LANES), 1)
    channel_ids = lax.broadcasted_iota(jnp.int32, (LANES, LANES), 0)
    for part in range(2):
        load_table(part).wait()

    def transform(first_segment):
        pieces = []
        for segment in range(first_segment, first_segment + 2):
            load_segment(segment).wait()
            begin = jnp.full((LANES, LANES), starts_ref[segment], jnp.int32)
            first = jnp.minimum(begin >> 7, (SLOT - CUT) // LANES)
            tiles = [slots_ref[segment, :, pl.ds(at, LANES)] for at in range(0, SLOT, LANES)]
            for bit, kept in ((4, CUT // LANES + 3), (2, CUT // LANES + 1), (1, CUT // LANES)):
                moved = (first & bit) != 0
                tiles = [jnp.where(moved, tiles[at + bit], tiles[at]) for at in range(kept)]
            place = lanes + (begin - first * LANES)
            stays = place < LANES
            place = place & (LANES - 1)
            turned = [jnp.take_along_axis(tile, place, axis=1, mode="promise_in_bounds") for tile in tiles]
            piece = [jnp.where(stays, turned[at], turned[at + 1]) for at in range(SEG // LANES)]
            pieces.append(jnp.concatenate(piece, 1) * window)
        piece = jnp.concatenate(pieces, 0)
        parts = []
        for parity in range(2):
            front, back = piece[:, :half], piece[:, half:]
            high, low = split(front + back if parity == 0 else front - back)
            stacked = jnp.concatenate([high, low, high], 1)
            rows = table_ref[pl.ds(parity * 2 * QUARTER, 2 * QUARTER), :]
            rows = jnp.concatenate([rows[:, :half], rows], 1)
            parts.append(dot(rows, stacked, ((1,), (1,))))
        power = jnp.concatenate(
            [part[:QUARTER] * part[:QUARTER] + part[QUARTER:] * part[QUARTER:] for part in parts], 0
        )
        smooth = dot(band_ref[...], jnp.concatenate(split(power), 0), ((1,), (0,)))
        scale = lax.rsqrt(smooth * (1.0 / (2 * HALF + 1)) + 1e-06)
        for parity in range(2):
            part_scale = scale[parity * QUARTER : (parity + 1) * QUARTER]
            for component in range(2):
                value = parts[parity][component * QUARTER : (component + 1) * QUARTER] * part_scale
                for second in range(2):
                    for which in range(2):
                        row = (which * 2 + 1 - parity) * TILE + component * SEGMENTS + first_segment + second
                        send_ref[pl.ds(row, OWNERS, stride=CHUNK), :] = value[
                            which * OWNERS : (which + 1) * OWNERS, second * LANES : (second + 1) * LANES
                        ]

    transform(0)
    transform(2)
    pl.semaphore_wait(row_sem, BLOCKS - 1)

    my_plane = my_inner & (PLANES - 1)
    my_side = my_inner >> 3

    def owner_of(block, side, plane):
        return (plane & 3) * (2 * BLOCKS) + block * 2 + side

    def send_rows(block, side, plane, first, count):
        return send_ref.at[pl.ds(pl.multiple_of(owner_of(block, side, plane) * CHUNK + first, TILE), count)]

    def recv_rows(slot, first, count):
        start = my_block * BLOCK_ROWS + (slot * 2 + my_side) * CHUNK + first
        return recv_ref.at[pl.ds(pl.multiple_of(start, TILE), count)]

    def send_step(step, _):
        block = (my_block + step) & (BLOCKS - 1)
        for turn in range(2):
            side = my_side ^ turn
            for ahead in (1, -1, 2, -2, 0):
                plane = (my_plane + ahead) & (PLANES - 1)
                if abs(ahead) < 2:
                    pieces = [(1 - ahead, 0, CHUNK)]
                else:
                    parity_row = 0 if ahead == 2 else TILE
                    pieces = [(3, parity_row, TILE), (3, parity_row + 2 * TILE, TILE)]

                def go():
                    for slot, first, count in pieces:
                        pltpu.make_async_remote_copy(
                            src_ref=send_rows(block, side, plane, first, count),
                            dst_ref=recv_rows(slot, first, count),
                            send_sem=send_sems.at[0],
                            recv_sem=recv_sems.at[step],
                            device_id=(block, side * PLANES + plane),
                            device_id_type=MESH,
                        ).start()

                if turn == 0 and ahead == 0:
                    pl.when(step > 0)(go)
                else:
                    go()
        return 0

    def shift_of(place):
        away = (place + 1) >> 1
        return jnp.where((place & 1) == 1, away, INNER - away) & (INNER - 1)

    def send_places(step, _):
        pltpu.make_async_remote_copy(
            src_ref=offsets_ref,
            dst_ref=places_ref.at[my_block],
            send_sem=send_sems.at[1],
            recv_sem=place_sems.at[step],
            device_id=((my_block + step) & (BLOCKS - 1), my_inner),
            device_id_type=MESH,
        ).start()
        return 0

    own_place = pltpu.make_async_copy(offsets_ref, places_ref.at[my_block], local_sems.at[1])
    own_place.start()
    own_chunk = pltpu.make_async_copy(
        send_rows(my_block, my_side, my_plane, 0, CHUNK), recv_rows(1, 0, CHUNK), local_sems.at[0]
    )
    own_chunk.start()
    lax.fori_loop(0, HEAD, send_step, 0)
    lax.fori_loop(1, BLOCKS, send_places, 0)
    lax.fori_loop(HEAD, BLOCKS, send_step, 0)

    next_device = (lax.rem(my_block + 1, BLOCKS), my_inner)

    def awaited(source, target, send_sem, recv_sem):
        return pltpu.make_async_remote_copy(
            src_ref=source,
            dst_ref=target,
            send_sem=send_sem,
            recv_sem=recv_sem,
            device_id=next_device,
            device_id_type=MESH,
        )

    real = lax.broadcasted_iota(jnp.int32, (TILE, TILE, LANES), 1) < SEGMENTS

    def block_of(step):
        return lax.rem(my_block + BLOCKS - step, BLOCKS)

    def block_values(block):
        values = recv_ref[pl.ds(pl.multiple_of(block * BLOCK_ROWS, BLOCK_ROWS), BLOCK_ROWS), :]
        return values.reshape(8, OWNED, TILE, LANES)

    def parts_of(value):
        flat = value.reshape(8 * TILE, LANES)
        high = flat.astype(jnp.bfloat16).astype(jnp.float32)
        return high, flat - high

    def receive(step):
        @pl.when(step == 0)
        def _():
            own_chunk.wait()
            own_place.wait()
            awaited(
                send_ref.at[pl.ds(0, BLOCK_ROWS - CHUNK)],
                recv_ref.at[pl.ds(0, BLOCK_ROWS - CHUNK)],
                send_sems.at[0],
                recv_sems.at[0],
            ).wait_recv()

        @pl.when(step > 0)
        def _():
            awaited(
                send_ref.at[pl.ds(0, BLOCK_ROWS)],
                recv_ref.at[pl.ds(0, BLOCK_ROWS)],
                send_sems.at[0],
                recv_sems.at[step],
            ).wait_recv()
            awaited(offsets_ref, places_ref.at[0], send_sems.at[1], place_sems.at[step]).wait_recv()

        values = block_values(block_of(step))
        for which in range(OWNED):
            high, low = parts_of(values[:, which])
            stacked = jnp.concatenate([high, high, low, low], 0).astype(jnp.bfloat16)

            def place_at(slot):
                right_ref[which, :, pl.ds(pl.multiple_of(slot * LANES, LANES), LANES)] = stacked

            place_at(BLOCKS + 1 - step)

            @pl.when(step < 2)
            def _():
                place_at(1 - step)

            @pl.when(step >= BLOCKS - 2)
            def _():
                place_at(BLOCKS + 1 - step + BLOCKS)

    def found_rows(step, pair):
        return found_ref.at[step, pl.ds(pl.multiple_of(pair * PARTS, PARTS), PARTS)]

    my_slot = (my_plane >> 2) * OWNERS + owner_of(my_block, my_side, my_plane)
    cross_rows = cross_ref.at[pl.ds(pl.multiple_of(my_slot * PARTS, PARTS), PARTS)]

    def correlate(step):
        block = block_of(step)
        values = block_values(block)
        offsets = places_ref[block]
        place = jnp.concatenate(
            [jnp.broadcast_to(offsets[pair : pair + 1], (PARTS, LANES)) for pair in range(PAIRS)], 0
        ).T + (channel_ids + SEP)
        lane = place & (LANES - 1)
        code = (place >> 7) * PARTS + (lanes & (PARTS - 1))
        picked = jnp.zeros((LANES, LANES), jnp.float32)
        columns = pl.ds(pl.multiple_of((BLOCKS - 1 - step) * LANES, LANES), SPAN * LANES)
        for which in range(OWNED):
            value = values[:, which]
            turned = pltpu.roll(value, SEGMENTS, 1)
            turned = jnp.where(real, turned, -turned)
            left = jnp.concatenate(
                [jnp.concatenate(parts_of(kind), 0).T.astype(jnp.bfloat16) for kind in (value, turned)], 0
            )
            gram = dot(jnp.concatenate([left, left], 1), right_ref[which, :, columns], ((1,), (0,)))
            for component in range(2):
                for near in range(SPAN):
                    tile = gram[
                        component * LANES : (component + 1) * LANES, near * LANES : (near + 1) * LANES
                    ]
                    value_there = jnp.take_along_axis(tile, lane, axis=1, mode="promise_in_bounds")
                    picked = jnp.where(code == near * PARTS + which * 2 + component, value_there, picked)
        found_ref[step] = picked.T

        def send_pair(shift, _):
            pair = (my_inner + shift_of(shift)) & (INNER - 1)
            pltpu.make_async_remote_copy(
                src_ref=found_rows(step, pair),
                dst_ref=cross_rows,
                send_sem=send_sems.at[2],
                recv_sem=cross_sem,
                device_id=(block, pair),
                device_id_type=MESH,
            ).start()
            return 0

        lax.fori_loop(1, INNER, send_pair, 0)

        @pl.when(step > 0)
        def _():
            send_pair(0, 0)

    def round_trip(turn, _):
        @pl.when(turn < BLOCKS)
        def _():
            receive(turn)

        @pl.when(turn >= 2 * REACH)
        def _():
            correlate(lax.rem(turn - REACH, BLOCKS))

        return 0

    lax.fori_loop(0, BLOCKS + 2 * REACH, round_trip, 0)

    own_cross = pltpu.make_async_copy(found_rows(0, my_inner), cross_rows, local_sems.at[2])
    own_cross.start()
    own_cross.wait()
    awaited(
        cross_ref.at[pl.ds(0, (DEVICES - 1) * PARTS)], cross_ref.at[pl.ds(0, (DEVICES - 1) * PARTS)], send_sems.at[2], cross_sem
    ).wait_recv()

    def summed(parity, component, which):
        part = (which * 2 + 1 - parity) * 2 + component
        return (
            cross_ref[pl.ds(part, OWNERS, stride=PARTS), :]
            + cross_ref[pl.ds(OWNERS * PARTS + part, OWNERS, stride=PARTS), :]
        )

    sums = []
    for parity in range(2):
        spectrum = jnp.concatenate(
            [summed(parity, component, which) for component in range(2) for which in range(2)], 0
        )
        high, low = split(spectrum)
        rows = table_ref[pl.ds(parity * 2 * QUARTER, 2 * QUARTER), :]
        table_high, table_low = rows[:, :half], rows[:, half:]
        first = ((0,), (0,))
        sums.append(dot(high, table_high, first) + (dot(high, table_low, first) + dot(low, table_high, first)))
    even, odd = sums
    shift = LAGS // 2
    segment_count = INNER * SEGMENTS
    factor = math.sqrt(segment_count / F) / segment_count
    out_ref[0, :, pl.ds(0, shift)] = (even - odd)[:, half - shift :] * factor
    out_ref[0, :, pl.ds(shift, shift)] = (even + odd)[:, :shift] * factor

    rest = DEVICES * ROWS - CHUNK
    awaited(send_ref.at[pl.ds(0, rest)], recv_ref.at[pl.ds(0, rest)], send_sems.at[0], recv_sems.at[0]).wait_send()
    awaited(
        places_ref.at[pl.ds(0, BLOCKS - 1)], places_ref.at[pl.ds(0, BLOCKS - 1)], send_sems.at[1], place_sems.at[0]
    ).wait_send()
    awaited(
        cross_ref.at[pl.ds(0, (DEVICES - 1) * PARTS)], cross_ref.at[pl.ds(0, (DEVICES - 1) * PARTS)], send_sems.at[2], cross_sem
    ).wait_send()


def local(records, starts, offsets):
    high, low = split_table()
    vmem = pl.BlockSpec(memory_space=pltpu.VMEM)
    hbm = pl.BlockSpec(memory_space=pltpu.HBM)
    dma = pltpu.SemaphoreType.DMA
    operands = (starts, offsets.T, records, jnp.asarray(high), jnp.asarray(low))
    return pl.pallas_call(
        kernel,
        out_shape=jax.ShapeDtypeStruct((1, LANES, LAGS), jnp.float32),
        in_specs=[hbm] * 5,
        out_specs=vmem,
        scratch_shapes=[
            pltpu.SMEM((SEGMENTS,), jnp.int32),
            pltpu.VMEM((PAIRS, LANES), jnp.int32),
            pltpu.VMEM((SEGMENTS, LANES, SLOT), jnp.float32),
            pltpu.VMEM((2 * F, SEG), jnp.bfloat16),
            pltpu.VMEM((F, 2 * F), jnp.bfloat16),
            pltpu.VMEM((DEVICES * ROWS, LANES), jnp.float32),
            pltpu.VMEM((DEVICES * ROWS, LANES), jnp.float32),
            pltpu.VMEM((BLOCKS, PAIRS, LANES), jnp.int32),
            pltpu.VMEM((OWNED, 2 * LANES, (BLOCKS + 2 * REACH) * LANES), jnp.bfloat16),
            pltpu.VMEM((BLOCKS, PAIRS * PARTS, LANES), jnp.float32),
            pltpu.VMEM((DEVICES * PARTS, LANES), jnp.float32),
            dma((2,)),
            dma((SEGMENTS,)),
            dma((2,)),
            dma((3,)),
            dma((3,)),
            dma((BLOCKS,)),
            dma((BLOCKS,)),
            dma,
            pltpu.SemaphoreType.REGULAR,
        ],
        compiler_params=pltpu.CompilerParams(
            collective_id=0, has_side_effects=True, vmem_limit_bytes=48 << 20
        ),
    )(*(pltpu.with_memory_space_constraint(value, pltpu.HBM) for value in operands))


def solution(mesh):
    placed = (P("blk", "inner", None), P("inner"), P("blk", None))
    return jax.shard_map(
        local, mesh=mesh, in_specs=placed, out_specs=P("inner", "blk", None), check_vma=False
    )
```

```python
import math

import ml_dtypes
import numpy as np

import jax
import jax.numpy as jnp
from jax import lax
from jax.experimental import pallas as pl
from jax.experimental.pallas import tpu as pltpu
from jax.sharding import PartitionSpec as P

SEG = 1024
SLOT = 2048
LAGS = 768
HALF = 32
PAIRS = 16
F = 512
SEP = 256
LANES = 128
CUT = SEG + LANES
BLOCKS = 16
INNER = 16
DEVICES = BLOCKS * INNER
SEGMENTS = 4
ROWS = 4 * SEGMENTS
HALF_ROWS = ROWS // 2
HEAD = 4
UNROLL = 16
QUARTER = F // 2
REACH = SEP // LANES
SPAN = 2 * REACH + 1
MESH = pl.DeviceIdType.MESH


def split_table():
    samples = np.arange(SEG // 2, dtype=np.int64)
    rows = []
    for parity in range(2):
        bins = 2 * np.arange(QUARTER, dtype=np.int64) + parity
        angle = 2.0 * np.pi / SEG * (bins[:, None] * samples[None, :] % SEG)
        rows += [np.cos(angle), -np.sin(angle)]
    table = np.concatenate(rows, 0).astype(np.float32)
    high = table.astype(ml_dtypes.bfloat16)
    low = (table - high.astype(np.float32)).astype(ml_dtypes.bfloat16)
    return high, low


def split(value):
    high = value.astype(jnp.bfloat16)
    low = (value - high.astype(jnp.float32)).astype(jnp.bfloat16)
    return high, low


def dot(left, right, dims):
    return lax.dot_general(left, right, (dims, ((), ())), preferred_element_type=jnp.float32)


def kernel(
    starts_hbm,
    offsets_hbm,
    records_ref,
    high_ref,
    low_ref,
    out_ref,
    starts_ref,
    offsets_ref,
    slots_ref,
    table_ref,
    band_ref,
    send_ref,
    recv_ref,
    place_ref,
    places_ref,
    right_ref,
    found_ref,
    cross_ref,
    index_ref,
    gram_ref,
    picked_ref,
    index_sems,
    load_sems,
    table_sems,
    local_sems,
    send_sems,
    recv_sems,
    place_sems,
    cross_sem,
    row_sem,
):
    my_block = lax.axis_index("blk")
    my_inner = lax.axis_index("inner")
    me = my_block * INNER + my_inner
    half = SEG // 2

    def load_table(part):
        source = (high_ref, low_ref)[part]
        return pltpu.make_async_copy(source, table_ref.at[:, pl.ds(part * half, half)], table_sems.at[part])

    def load_segment(segment):
        return pltpu.make_async_copy(records_ref.at[:, segment, :], slots_ref.at[segment], load_sems.at[segment])

    load_starts = pltpu.make_async_copy(starts_hbm, starts_ref, index_sems.at[0])
    load_offsets = pltpu.make_async_copy(offsets_hbm, offsets_ref, index_sems.at[1])
    load_starts.start()
    load_offsets.start()
    for segment in range(2):
        load_segment(segment).start()
    for part in range(2):
        load_table(part).start()
    for segment in range(2, SEGMENTS):
        load_segment(segment).start()

    barrier = pltpu.get_barrier_semaphore()

    def peer_in_row(step):
        return (my_block, (my_inner + step) & (INNER - 1))

    def peer_in_column(step):
        return ((my_block + step) & (BLOCKS - 1), my_inner)

    def greet(step, _):
        pl.semaphore_signal(barrier, inc=1, device_id=peer_in_row(step), device_id_type=MESH)
        pl.semaphore_signal(barrier, inc=1, device_id=peer_in_column(step), device_id_type=MESH)
        return 0

    lax.fori_loop(1, INNER, greet, 0)

    pl.semaphore_wait(barrier, 2 * (INNER - 1))

    def pass_on(step, _):
        pl.semaphore_signal(row_sem, inc=1, device_id=peer_in_column(step), device_id_type=MESH)
        return 0

    lax.fori_loop(1, BLOCKS, pass_on, 0)

    load_offsets.wait()
    channel_ids = lax.broadcasted_iota(jnp.int32, (1, LANES), 1)
    for pair in range(PAIRS):
        row = offsets_ref[pl.ds(pair, 1), :] + (channel_ids + SEP)
        place_ref[pl.ds(4 * pair, 4), :] = jnp.broadcast_to(row, (4, LANES))

    gap = 2 * (
        lax.broadcasted_iota(jnp.int32, (QUARTER, QUARTER), 0) - lax.broadcasted_iota(jnp.int32, (QUARTER, QUARTER), 1)
    )

    def near_bins(shift):
        distance = jnp.abs(gap + shift)
        distance = jnp.minimum(distance, F - distance)
        return jnp.where(distance <= HALF, 1.0, 0.0).astype(jnp.bfloat16)

    same, after, before = near_bins(0), near_bins(1), near_bins(-1)
    for copy in range(2):
        band_ref[pl.ds(0, QUARTER), pl.ds(copy * F, QUARTER)] = same
        band_ref[pl.ds(0, QUARTER), pl.ds(copy * F + QUARTER, QUARTER)] = before
        band_ref[pl.ds(QUARTER, QUARTER), pl.ds(copy * F, QUARTER)] = after
        band_ref[pl.ds(QUARTER, QUARTER), pl.ds(copy * F + QUARTER, QUARTER)] = same
    samples = lax.broadcasted_iota(jnp.int32, (8, SEG), 1).astype(jnp.float32)
    window = (0.5 - 0.5 * jnp.cos(2.0 * jnp.pi / SEG * samples))[:1]
    load_starts.wait()
    lanes = lax.broadcasted_iota(jnp.int32, (LANES, LANES), 1)
    for part in range(2):
        load_table(part).wait()

    def transform(first_segment):
        pieces = []
        for segment in range(first_segment, first_segment + 2):
            load_segment(segment).wait()
            begin = jnp.full((LANES, LANES), starts_ref[segment], jnp.int32)
            first = jnp.minimum(begin >> 7, (SLOT - CUT) // LANES)
            tiles = [slots_ref[segment, :, pl.ds(at, LANES)] for at in range(0, SLOT, LANES)]
            for bit, kept in ((4, CUT // LANES + 3), (2, CUT // LANES + 1), (1, CUT // LANES)):
                moved = (first & bit) != 0
                tiles = [jnp.where(moved, tiles[at + bit], tiles[at]) for at in range(kept)]
            place = lanes + (begin - first * LANES)
            stays = place < LANES
            place = place & (LANES - 1)
            turned = [jnp.take_along_axis(tile, place, axis=1, mode="promise_in_bounds") for tile in tiles]
            piece = [jnp.where(stays, turned[at], turned[at + 1]) for at in range(SEG // LANES)]
            pieces.append(jnp.concatenate(piece, 1) * window)
        piece = jnp.concatenate(pieces, 0)
        parts = []
        for parity in range(2):
            front, back = piece[:, :half], piece[:, half:]
            high, low = split(front + back if parity == 0 else front - back)
            stacked = jnp.concatenate([high, low, high], 1)
            rows = table_ref[pl.ds(parity * 2 * QUARTER, 2 * QUARTER), :]
            rows = jnp.concatenate([rows[:, :half], rows], 1)
            parts.append(dot(rows, stacked, ((1,), (1,))))
        power = jnp.concatenate(
            [part[:QUARTER] * part[:QUARTER] + part[QUARTER:] * part[QUARTER:] for part in parts], 0
        )
        smooth = dot(band_ref[...], jnp.concatenate(split(power), 0), ((1,), (0,)))
        scale = lax.rsqrt(smooth * (1.0 / (2 * HALF + 1)) + 1e-06)
        for parity in range(2):
            part_scale = scale[parity * QUARTER : (parity + 1) * QUARTER]
            for component in range(2):
                value = parts[parity][component * QUARTER : (component + 1) * QUARTER] * part_scale
                for second in range(2):
                    row = first_segment // 2 * HALF_ROWS + (parity * 2 + component) * 2 + second
                    send_ref[pl.ds(row, QUARTER, stride=ROWS), :] = value[:, second * LANES : (second + 1) * LANES]

    transform(0)
    pl.semaphore_wait(row_sem, BLOCKS - 1)

    def chunk(device):
        return pl.ds(pl.multiple_of(device * ROWS, ROWS), ROWS)

    def part_of_chunk(device, first, count):
        return pl.ds(pl.multiple_of(device * ROWS + first, HALF_ROWS), count)

    def shift_of(place):
        away = (place + 1) >> 1
        return jnp.where((place & 1) == 1, away, INNER - away) & (INNER - 1)

    def send_step(step, first, count):
        block = (my_block + step) & (BLOCKS - 1)

        def send_one(place, _):
            other = (my_inner + shift_of(place)) & (INNER - 1)
            pltpu.make_async_remote_copy(
                src_ref=send_ref.at[part_of_chunk(block * INNER + other, first, count)],
                dst_ref=recv_ref.at[part_of_chunk(me, first, count)],
                send_sem=send_sems.at[0],
                recv_sem=recv_sems.at[step],
                device_id=(block, other),
                device_id_type=MESH,
            ).start()
            return 0

        lax.fori_loop(1, INNER, send_one, 0)

        @pl.when(step > 0)
        def _():
            send_one(0, 0)

    def send_places(step, _):
        pltpu.make_async_remote_copy(
            src_ref=place_ref,
            dst_ref=places_ref.at[my_block],
            send_sem=send_sems.at[1],
            recv_sem=place_sems.at[step],
            device_id=((my_block + step) & (BLOCKS - 1), my_inner),
            device_id_type=MESH,
        ).start()
        return 0

    def sends(first_step, last_step, first, count):
        def one_step(step, _):
            send_step(step, first, count)
            return 0

        lax.fori_loop(first_step, last_step, one_step, 0)

    own_place = pltpu.make_async_copy(place_ref, places_ref.at[my_block], local_sems.at[1])
    own_place.start()
    sends(0, HEAD, 0, HALF_ROWS)
    transform(2)
    own_chunk = pltpu.make_async_copy(send_ref.at[chunk(me)], recv_ref.at[chunk(me)], local_sems.at[0])
    own_chunk.start()
    sends(0, HEAD, HALF_ROWS, HALF_ROWS)
    lax.fori_loop(1, BLOCKS, send_places, 0)
    sends(HEAD, BLOCKS, 0, ROWS)

    next_device = (lax.rem(my_block + 1, BLOCKS), my_inner)

    def awaited(source, target, send_sem, recv_sem):
        return pltpu.make_async_remote_copy(
            src_ref=source,
            dst_ref=target,
            send_sem=send_sem,
            recv_sem=recv_sem,
            device_id=next_device,
            device_id_type=MESH,
        )

    block_rows = INNER * ROWS
    places8 = lax.broadcasted_iota(jnp.int32, (INNER, HALF_ROWS, LANES), 1)
    lower = places8 < HALF_ROWS // 2
    real = places8 & 2 == 0

    def block_of(step):
        return lax.rem(my_block + BLOCKS - step, BLOCKS)

    def block_values(block):
        values = recv_ref[pl.ds(pl.multiple_of(block * block_rows, block_rows), block_rows), :]
        values = values.reshape(INNER, ROWS, LANES)
        early, late = values[:, :HALF_ROWS], values[:, HALF_ROWS:]
        turn = HALF_ROWS // 2
        return (
            jnp.where(lower, early, pltpu.roll(late, turn, 1)),
            jnp.where(lower, pltpu.roll(early, turn, 1), late),
        )

    def receive(step):
        @pl.when(step == 0)
        def _():
            own_chunk.wait()
            own_place.wait()
            awaited(
                send_ref.at[pl.ds(0, block_rows - ROWS)],
                recv_ref.at[pl.ds(0, block_rows - ROWS)],
                send_sems.at[0],
                recv_sems.at[0],
            ).wait_recv()

        @pl.when(step > 0)
        def _():
            awaited(
                send_ref.at[pl.ds(0, block_rows)],
                recv_ref.at[pl.ds(0, block_rows)],
                send_sems.at[0],
                recv_sems.at[step],
            ).wait_recv()
            awaited(place_ref, places_ref.at[0], send_sems.at[1], place_sems.at[step]).wait_recv()

        values = block_values(block_of(step))
        for parity in range(2):
            value = values[parity].reshape(LANES, LANES)
            high, low = split(value)
            stacked = jnp.concatenate([high, low, high], 0)

            def place_at(slot):
                right_ref[parity, :, pl.ds(pl.multiple_of(slot * LANES, LANES), LANES)] = stacked

            place_at(BLOCKS + 1 - step)

            @pl.when(step < 2)
            def _():
                place_at(1 - step)

            @pl.when(step >= BLOCKS - 2)
            def _():
                place_at(BLOCKS + 1 - step + BLOCKS)

    def correlate(step):
        block = block_of(step)
        values = block_values(block)
        place = jnp.concatenate([places_ref[block], jnp.zeros((LANES - 4 * PAIRS, LANES), jnp.int32)], 0).T
        index_ref[...] = place
        columns = pl.ds(pl.multiple_of((BLOCKS - 1 - step) * LANES, LANES), SPAN * LANES)
        for parity in range(2):
            value = values[parity]
            turned = jnp.where(real, pltpu.roll(value, HALF_ROWS - 2, 1), -pltpu.roll(value, 2, 1))
            left = jnp.concatenate([value.reshape(LANES, LANES).T, turned.reshape(LANES, LANES).T], 0)
            high, low = split(left)
            gram_ref[pl.ds(parity * 2 * LANES, 2 * LANES), :] = dot(
                jnp.concatenate([high, high, low], 1), right_ref[parity, :, columns], ((1,), (0,))
            )
        part_lanes = lanes[:8] & 3

        def pick(group, _):
            rows = pl.ds(pl.multiple_of(group * 8, 8), 8)
            place = index_ref[rows, :]
            lane = place & (LANES - 1)
            code = (place >> 7) * 4 + part_lanes
            picked = jnp.zeros((8, LANES), jnp.float32)
            for part in range(4):
                for near in range(SPAN):
                    source = pl.ds(pl.multiple_of(part * LANES + group * 8, 8), 8)
                    value_there = jnp.take_along_axis(
                        gram_ref[source, pl.ds(near * LANES, LANES)], lane, axis=1, mode="promise_in_bounds"
                    )
                    picked = jnp.where(code == near * 4 + part, value_there, picked)
            picked_ref[rows, :] = picked
            return 0

        lax.fori_loop(0, LANES // 8, pick, 0, unroll=UNROLL)
        picked = picked_ref[...].T
        for pair in range(PAIRS):
            found_ref[step, pair] = picked[4 * pair : 4 * pair + 4]

        def send_pair(shift, _):
            pair = (my_inner + shift_of(shift)) & (INNER - 1)
            pltpu.make_async_remote_copy(
                src_ref=found_ref.at[step, pair],
                dst_ref=cross_ref.at[me],
                send_sem=send_sems.at[2],
                recv_sem=cross_sem,
                device_id=(block, pair),
                device_id_type=MESH,
            ).start()
            return 0

        lax.fori_loop(1, INNER, send_pair, 0)

        @pl.when(step > 0)
        def _():
            send_pair(0, 0)

    def round_trip(turn, _):
        @pl.when(turn < BLOCKS)
        def _():
            receive(turn)

        @pl.when(turn >= 2 * REACH)
        def _():
            correlate(lax.rem(turn - REACH, BLOCKS))

        return 0

    lax.fori_loop(0, BLOCKS + 2 * REACH, round_trip, 0)

    own_cross = pltpu.make_async_copy(found_ref.at[0, my_inner], cross_ref.at[me], local_sems.at[2])
    own_cross.start()
    own_cross.wait()
    awaited(
        cross_ref.at[pl.ds(0, DEVICES - 1)], cross_ref.at[pl.ds(0, DEVICES - 1)], send_sems.at[2], cross_sem
    ).wait_recv()

    sums = []
    for parity in range(2):
        spectrum = jnp.concatenate([cross_ref[:, parity * 2 + component, :] for component in range(2)], 0)
        high, low = split(spectrum)
        rows = table_ref[pl.ds(parity * 2 * QUARTER, 2 * QUARTER), :]
        table_high, table_low = rows[:, :half], rows[:, half:]
        sums.append(
            dot(
                jnp.concatenate([high, high, low], 0),
                jnp.concatenate([table_high, table_low, table_high], 0),
                ((0,), (0,)),
            )
        )
    even, odd = sums
    shift = LAGS // 2
    segment_count = INNER * SEGMENTS
    factor = math.sqrt(segment_count / F) / segment_count
    out_ref[0, :, pl.ds(0, shift)] = (even - odd)[:, half - shift :] * factor
    out_ref[0, :, pl.ds(shift, shift)] = (even + odd)[:, :shift] * factor

    rest = DEVICES * ROWS - ROWS
    awaited(send_ref.at[pl.ds(0, rest)], recv_ref.at[pl.ds(0, rest)], send_sems.at[0], recv_sems.at[0]).wait_send()
    awaited(
        places_ref.at[pl.ds(0, BLOCKS - 1)], places_ref.at[pl.ds(0, BLOCKS - 1)], send_sems.at[1], place_sems.at[0]
    ).wait_send()
    awaited(
        cross_ref.at[pl.ds(0, DEVICES - 1)], cross_ref.at[pl.ds(0, DEVICES - 1)], send_sems.at[2], cross_sem
    ).wait_send()


def local(records, starts, offsets):
    high, low = split_table()
    vmem = pl.BlockSpec(memory_space=pltpu.VMEM)
    hbm = pl.BlockSpec(memory_space=pltpu.HBM)
    dma = pltpu.SemaphoreType.DMA
    operands = (starts, offsets.T, records, jnp.asarray(high), jnp.asarray(low))
    return pl.pallas_call(
        kernel,
        out_shape=jax.ShapeDtypeStruct((1, LANES, LAGS), jnp.float32),
        in_specs=[hbm] * 5,
        out_specs=vmem,
        scratch_shapes=[
            pltpu.SMEM((SEGMENTS,), jnp.int32),
            pltpu.VMEM((PAIRS, LANES), jnp.int32),
            pltpu.VMEM((SEGMENTS, LANES, SLOT), jnp.float32),
            pltpu.VMEM((2 * F, SEG), jnp.bfloat16),
            pltpu.VMEM((F, 2 * F), jnp.bfloat16),
            pltpu.VMEM((DEVICES * ROWS, LANES), jnp.float32),
            pltpu.VMEM((DEVICES * ROWS, LANES), jnp.float32),
            pltpu.VMEM((4 * PAIRS, LANES), jnp.int32),
            pltpu.VMEM((BLOCKS, 4 * PAIRS, LANES), jnp.int32),
            pltpu.VMEM((2, 3 * LANES, (BLOCKS + 2 * REACH) * LANES), jnp.bfloat16),
            pltpu.VMEM((BLOCKS, PAIRS, 4, LANES), jnp.float32),
            pltpu.VMEM((DEVICES, 4, LANES), jnp.float32),
            pltpu.VMEM((LANES, LANES), jnp.int32),
            pltpu.VMEM((4 * LANES, SPAN * LANES), jnp.float32),
            pltpu.VMEM((LANES, LANES), jnp.float32),
            dma((2,)),
            dma((SEGMENTS,)),
            dma((2,)),
            dma((3,)),
            dma((3,)),
            dma((BLOCKS,)),
            dma((BLOCKS,)),
            dma,
            pltpu.SemaphoreType.REGULAR,
        ],
        compiler_params=pltpu.CompilerParams(
            collective_id=0, has_side_effects=True, vmem_limit_bytes=48 << 20
        ),
    )(*(pltpu.with_memory_space_constraint(value, pltpu.HBM) for value in operands))


def solution(mesh):
    placed = (P("blk", "inner", None), P("inner"), P("blk", None))
    return jax.shard_map(
        local, mesh=mesh, in_specs=placed, out_specs=P("inner", "blk", None), check_vma=False
    )
```
